512 devices in a mesh: row: 128 (over y, z, core), col: 4 (over x).
Axes of the slice: x: 4, y: 8, z: 8, core: 2. Of those that a mesh axis runs over, the one named last changes fastest.
Arguments:
- feat_in: bfloat16 [4096, 256, 256], P('row', 'col'), may hold values from -6 to 6
- conv_weight: bfloat16 [2304, 256], P('col'), may hold values from -0.125 to 0.125
- conv_bias: float32 [256], replicated, may hold values from -4 to 4
- proj_weight: bfloat16 [256, 768], replicated, may hold values from -0.375 to 0.375
- qkv_weight: bfloat16 [768, 2304], P('row'), may hold values from -2 to 2
- tissue: int32 [2048, 128], P('row', 'col'), may hold values from 0 to 1, as said below
- phase: int32 [2048, 128], P('row', 'col'), may hold values from 0 to 3, as said below
Outputs:
- attended: bfloat16 [2048, 128, 768], P('row', 'col')
The draws below stay inside these ranges and needn't reach their ends.
Inputs may be any that keep to these rules, and one draw needn't show every extreme that they name: Within each column strip, phase is the token column plus an offset drawn for each token row, modulo 4. In each device's block of tokens, every phase holds at least one tissue token.
All inputs are finite; a program needn't handle non-finite values.
Results may differ from the reference program's by a relative error of at most 0.0065.
Values may be sent and summed in bfloat16 or wider, within the bound.
A program may use at most 64 MiB of HBM per device.

```python
import jax
import jax.numpy as jnp
from jax import lax

C = 256
HEADS = 12
HD = 64
D = 768
DILATION_STEP = 4
LOCAL_ROWS = 16
LOCAL_COLUMNS = 32
GROUP = 1024
SLIDE_ROWS = 2048
SLIDE_COLUMNS = 128
N_COL = 4


def draw_phase(key, part):
    strip_count = SLIDE_COLUMNS // LOCAL_COLUMNS
    row_offsets = jax.random.randint(jax.random.fold_in(key, 13), (SLIDE_ROWS, strip_count), 0, DILATION_STEP, dtype=jnp.int32)
    spread_rows = jnp.repeat(row_offsets, LOCAL_COLUMNS, axis=1)
    column_indices = jnp.arange(SLIDE_COLUMNS, dtype=jnp.int32)[None, :] % LOCAL_COLUMNS
    return ((column_indices + spread_rows) % DILATION_STEP).astype(jnp.int32)


def draw_tissue(key, part):
    band_count = SLIDE_ROWS // LOCAL_ROWS
    band_index = jnp.arange(SLIDE_ROWS, dtype=jnp.int32) // LOCAL_ROWS
    edge_dist = jnp.minimum(band_index, band_count - 1 - band_index)
    threshold = 10 + 170 * edge_dist // band_count
    random_ints = jax.random.randint(jax.random.fold_in(key, 11), (SLIDE_ROWS, SLIDE_COLUMNS), 0, 100, dtype=jnp.int32)
    row_positions = jnp.arange(SLIDE_ROWS, dtype=jnp.int32)[:, None]
    column_positions = jnp.arange(SLIDE_COLUMNS, dtype=jnp.int32)[None, :]
    forced_flags = (row_positions % LOCAL_ROWS == 0) & (column_positions % LOCAL_COLUMNS < DILATION_STEP)
    tissue_live = (random_ints < threshold[:, None]) | forced_flags
    return tissue_live.astype(jnp.int32)


def draw_qkv_weight(key, part):
    basic_draw = jax.random.normal(jax.random.fold_in(key, 3), (D, 3 * D), jnp.float32) * D ** (-0.5)
    return jnp.clip(basic_draw, -2.0, 2.0).astype(jnp.bfloat16)


def steps_of(stream_key, extent, cuts, smallest, top_value):
    def one(position, shards_of):
        heights = jax.random.uniform(jax.random.fold_in(jax.random.fold_in(stream_key, 6), position), (shards_of,), jnp.float32, smallest / len(cuts), top_value / len(cuts))
        return jnp.repeat(jnp.exp(heights), extent[position] // shards_of).reshape((-1,) + (1,) * (len(extent) - position - 1))

    factor_of = one(*cuts[0])
    for cut in cuts[1:]:
        factor_of = factor_of * one(*cut)
    return factor_of


def gaussian(rng, dims, deviation, bound, split=(), held_as=jnp.bfloat16):
    factor_of = steps_of(rng, dims, split, -0.22, 0.18) if split else 1.0
    values = jax.random.normal(rng, dims, jnp.float32) * deviation * factor_of
    return jnp.minimum(jnp.maximum(values, -bound), bound).astype(held_as)


def setup_inputs(seed: int = 0) -> dict:
    key_list = jax.random.split(jax.random.key(seed), 8)
    return {
        "feat_in": gaussian(key_list[0], (2 * SLIDE_ROWS, 2 * SLIDE_COLUMNS, C), 1.0, 6.0, ((0, 128), (1, 4))),
        "conv_weight": gaussian(key_list[1], (9 * C, C), (9 * C) ** -0.5, 0.125, ((0, 4),)),
        "conv_bias": gaussian(key_list[2], (C,), 0.7, 4.0, (), jnp.float32),
        "proj_weight": gaussian(key_list[3], (C, D), C ** -0.5, 0.375),
        "qkv_weight": draw_qkv_weight(jax.random.fold_in(key_list[7], 71), 0),
        "tissue": draw_tissue(jax.random.fold_in(key_list[7], 71), 0),
        "phase": draw_phase(jax.random.fold_in(key_list[7], 71), 0),
    }


def layer_norm(values):
    centred = values - lax.optimization_barrier(jnp.mean(values, axis=-1, keepdims=True))
    spread_rows = lax.optimization_barrier(jnp.mean(centred * centred, axis=-1, keepdims=True))
    return centred * lax.rsqrt(spread_rows + 1e-05)

def group_attention(operands):
    qkv_group, tissue_group = operands
    queries = qkv_group[:, :D].reshape(GROUP, HEADS, HD).astype(jnp.float32)
    keys_all = qkv_group[:, D:2 * D].reshape(GROUP, HEADS, HD).astype(jnp.float32)
    values_all = qkv_group[:, 2 * D:].reshape(GROUP, HEADS, HD).astype(jnp.float32)
    scores = jnp.einsum('qhd,khd->hqk', queries, keys_all) * HD ** (-0.5)
    allowed = (tissue_group > 0)[None, None, :]
    scores = jnp.where(allowed, scores, -1e+30)
    top_score = lax.optimization_barrier(jnp.max(scores, axis=-1, keepdims=True))
    weights = jnp.where(allowed, jnp.exp(scores - top_score), 0.0)
    denominator = lax.optimization_barrier(jnp.sum(weights, axis=-1))
    rounded = weights.astype(jnp.bfloat16).astype(jnp.float32)
    mixed_heads = jnp.einsum('hqk,khd->qhd', rounded, values_all) / jnp.transpose(denominator)[:, :, None]
    mixed_heads = mixed_heads * tissue_group.astype(jnp.float32)[:, None, None]
    return mixed_heads.reshape(GROUP, D).astype(jnp.bfloat16)

def reference(feat_in, conv_weight, conv_bias, proj_weight, qkv_weight, tissue, phase):
    padded = jnp.pad(feat_in, ((1, 0), (1, 0), (0, 0)))
    summed = jnp.zeros((SLIDE_ROWS * SLIDE_COLUMNS, C), jnp.float32)
    for row_tap in range(3):
        for col_tap in range(3):
            window = padded[row_tap:row_tap + 2 * SLIDE_ROWS - 1:2, col_tap:col_tap + 2 * SLIDE_COLUMNS - 1:2, :]
            offset = (3 * row_tap + col_tap) * C
            summed = summed + jnp.dot(window.reshape(SLIDE_ROWS * SLIDE_COLUMNS, C), conv_weight[offset:offset + C], preferred_element_type=jnp.float32)
    features = jax.nn.gelu(summed + conv_bias).astype(jnp.bfloat16)
    strip_feat = features.reshape(SLIDE_ROWS, N_COL, LOCAL_COLUMNS, C).transpose(1, 0, 2, 3).reshape(N_COL, SLIDE_ROWS * LOCAL_COLUMNS, C)
    segment_per_row = (jnp.arange(SLIDE_ROWS, dtype=jnp.int32) // (2 * DILATION_STEP * LOCAL_ROWS)).astype(jnp.int32)
    group_labels = (segment_per_row[:, None] * DILATION_STEP + phase).astype(jnp.int32)
    strip_group = group_labels.reshape(SLIDE_ROWS, N_COL, LOCAL_COLUMNS).transpose(1, 0, 2).reshape(N_COL, SLIDE_ROWS * LOCAL_COLUMNS)
    strip_tissue = tissue.reshape(SLIDE_ROWS, N_COL, LOCAL_COLUMNS).transpose(1, 0, 2).reshape(N_COL, SLIDE_ROWS * LOCAL_COLUMNS)

    def strip_output(operands):
        feat_strip, group_strip, tissue_strip = operands
        projected = jnp.dot(feat_strip, proj_weight, preferred_element_type=jnp.float32)
        tokens_bf = layer_norm(projected).astype(jnp.bfloat16)
        qkv_all = jnp.dot(tokens_bf, qkv_weight, preferred_element_type=jnp.float32).astype(jnp.bfloat16)
        ordering = jnp.argsort(group_strip, stable=True).astype(jnp.int32)
        sorted_qkv = qkv_all[ordering].reshape(-1, GROUP, 3 * D)
        sorted_tissue = tissue_strip[ordering].reshape(-1, GROUP)
        attended_sorted = lax.map(group_attention, (sorted_qkv, sorted_tissue))
        return jnp.zeros((SLIDE_ROWS * LOCAL_COLUMNS, D), jnp.bfloat16).at[ordering].set(attended_sorted.reshape(-1, D))
    strips = lax.map(strip_output, (strip_feat, strip_group, strip_tissue))
    return strips.reshape(N_COL, SLIDE_ROWS, LOCAL_COLUMNS, D).transpose(1, 0, 2, 3).reshape(SLIDE_ROWS, SLIDE_COLUMNS, D)
```

```python
import jax
import jax.numpy as jnp
from jax import lax
from jax.experimental import pallas as pl
from jax.experimental.pallas import tpu as pltpu
from jax.sharding import PartitionSpec as P

MESH = pl.DeviceIdType.MESH
F32 = jnp.float32
BF16 = jnp.bfloat16
ROWS = 128
COLS = 4
PLANE = 16
NY = 8
HALF = 1152
VMEM_LIMIT = 56 * 1024 * 1024


def iota(shape, dim):
    return lax.broadcasted_iota(jnp.int32, shape, dim)


def onehot(cond):
    return jnp.where(cond, 1.0, 0.0)


def dot(a, b):
    return jnp.dot(a, b, preferred_element_type=F32)


def dot_nt(a, b):
    return lax.dot_general(a, b, (((1,), (1,)), ((), ())), preferred_element_type=F32)


def dot_tn(a, b):
    return lax.dot_general(a, b, (((0,), (0,)), ((), ())), preferred_element_type=F32)


def remote(src, dst, send_sem, recv_sem, device):
    return pltpu.make_async_remote_copy(
        src_ref=src,
        dst_ref=dst,
        send_sem=send_sem,
        recv_sem=recv_sem,
        device_id=device,
        device_id_type=MESH,
    )


def greet(devices):
    barrier = pltpu.get_barrier_semaphore()
    for device in devices:
        pl.semaphore_signal(barrier, inc=1, device_id=device, device_id_type=MESH)
    pl.semaphore_wait(barrier, len(devices))


def conv_kernel(
    feat, cw, bias, w8, phase, tissue, fs, wc,
    grid_in, ext, halo, top, cwg, wsend, wz,
    cw_send, cw_recv, h_send, h_recv, z_send, z_recv, own_sem,
):
    row, col = lax.axis_index("row"), lax.axis_index("col")
    core = lax.rem(row, 2)
    base = row - lax.rem(row, PLANE)
    mine = row - base
    sibling = (base + lax.rem(mine, PLANE) + 1 - 2 * core, col)
    right, left = lax.rem(col + 1, COLS), lax.rem(col + COLS - 1, COLS)
    down, up = lax.rem(row + 1, ROWS), lax.rem(row + ROWS - 1, ROWS)
    plane = [(base + lax.rem(mine + k, PLANE), col) for k in range(1, PLANE)]
    greet(
        [(row, right), (row, left), (down, col), (up, col), (down, right), (up, left)]
        + plane
    )

    part = pl.multiple_of(core * 288, 32)

    def cw_piece(slot, start, size):
        return cwg.at[slot, pl.ds(pl.multiple_of(part + start, 16), size), :]

    across = lax.rem(col + 2, COLS)
    own = pltpu.make_async_copy(cw, cwg.at[col], own_sem)
    own.start()
    half = cw.at[pl.ds(part, 288), :]
    to_right = remote(half, cw_piece(col, 0, 288), cw_send.at[0], cw_recv.at[0], (row, right))
    to_left = remote(half, cw_piece(col, 0, 288), cw_send.at[1], cw_recv.at[1], (row, left))
    to_right.start()
    to_left.start()

    top_copy = remote(feat.at[31], top, h_send.at[0], h_recv.at[0], (down, col))
    top_copy.start()

    for c in range(2):
        for j in range(3):
            wsend[c, :, 384 * j : 384 * j + 384] = w8[
                :, 768 * j + 384 * c : 768 * j + 384 * c + 384
            ]
    z_copies = []
    for k in range(1, PLANE):
        to_core = lax.rem(core + k, 2)
        copy = remote(
            wsend.at[to_core], wz.at[mine], z_send.at[k], z_recv.at[k], plane[k - 1]
        )
        copy.start()
        z_copies.append(copy)
    own_z = pltpu.make_async_copy(wsend.at[core], wz.at[mine], z_recv.at[0])
    own_z.start()

    o, c = iota((256, 256), 0), iota((256, 256), 1)
    k, si, sp = o & 7, (o >> 3) & 3, (o >> 5) & 1
    r = 2 * ((o >> 6) & 1) + (o >> 7)
    split = onehot(c == r * 64 + 8 * k + 2 * si + sp).astype(BF16)
    for g in range(8):
        x = feat[4 * g : 4 * g + 4].reshape(256, 256)
        y = dot(split, x).reshape(2, 2, 2, 4, 8, 256)
        grid_in[0, 2 * g : 2 * g + 2, 0, 0:4] = y[0, :, 0]
        grid_in[0, 2 * g : 2 * g + 2, 1, 1:5] = y[0, :, 1]
        grid_in[1, 2 * g + 1 : 2 * g + 3, 0, 0:4] = y[1, :, 0]
        grid_in[1, 2 * g + 1 : 2 * g + 3, 1, 1:5] = y[1, :, 1]

    for rp in range(2):
        for i in range(0, 16, 8):
            rows8 = [grid_in[rp, rp + i + e, 1, 4, 7:8, :] for e in range(8)]
            ext[16 * rp + i : 16 * rp + i + 8, :] = jnp.concatenate(rows8, axis=0).astype(BF16)
    left_copy = remote(ext, halo.at[0:32], h_send.at[1], h_recv.at[1], (row, right))
    left_copy.start()
    corner_copy = remote(
        ext.at[24:32], halo.at[32:40], h_send.at[2], h_recv.at[2], (down, right)
    )
    corner_copy.start()

    to_right.wait_recv()
    on_right = remote(
        cw_piece(left, 0, 144), cw_piece(left, 0, 144), cw_send.at[2], cw_recv.at[2], (row, right)
    )
    on_right.start()
    sib_left = remote(
        cw_piece(left, 0, 288), cw_piece(left, 0, 288), cw_send.at[4], cw_recv.at[4], sibling
    )
    sib_left.start()
    to_left.wait_recv()
    on_left = remote(
        cw_piece(right, 144, 144), cw_piece(right, 144, 144), cw_send.at[3], cw_recv.at[3], (row, left)
    )
    on_left.start()
    sib_right = remote(
        cw_piece(right, 0, 288), cw_piece(right, 0, 288), cw_send.at[5], cw_recv.at[5], sibling
    )
    sib_right.start()

    top_copy.wait_recv()
    left_copy.wait_recv()
    corner_copy.wait_recv()
    below = row > 0
    inner = col > 0
    o, c = iota((64, 64), 0), iota((64, 64), 1)
    split_row = onehot(c == 8 * (o & 7) + 2 * ((o >> 3) & 3) + (o >> 5)).astype(BF16)
    yt = jnp.where(below, dot(split_row, top[...]), 0.0).reshape(2, 4, 8, 256)
    grid_in[1, 0, 0, 0:4] = yt[0]
    grid_in[1, 0, 1, 1:5] = yt[1]
    o, c = iota((272, 40), 0), iota((272, 40), 1)
    source = o >> 3
    source = jnp.where(source < 16, source, jnp.where(source == 16, 39, source - 1))
    spread = onehot((c == source) & ((o & 7) == 0)).astype(BF16)
    edge = jnp.where(inner, dot(spread, halo[...]), 0.0).reshape(34, 8, 256)
    first = iota((1, 8, 256), 1) == 0
    moved = pltpu.roll(grid_in[0, 0:16, 1, 4], 1, 1)
    grid_in[0, 0:16, 1, 0] = jnp.where(first, edge[0:16], moved)
    grid_in[0, 16, 1, 0] = jnp.zeros((8, 256), F32)
    moved = pltpu.roll(grid_in[1, 0:17, 1, 4], 1, 1)
    keep = edge[16:33]
    keep = jnp.where((iota((17, 8, 256), 0) == 0) & jnp.logical_not(below), 0.0, keep)
    grid_in[1, 0:17, 1, 0] = jnp.where(first, keep, moved)

    on_right.wait_recv()
    sib_on = remote(
        cw_piece(across, 0, 144), cw_piece(across, 0, 144), cw_send.at[6], cw_recv.at[6], sibling
    )
    sib_on.start()
    on_left.wait_recv()
    sib_off = remote(
        cw_piece(across, 144, 144), cw_piece(across, 144, 144), cw_send.at[7], cw_recv.at[7], sibling
    )
    sib_off.start()
    own.wait()
    for copy in (sib_left, sib_right, sib_on, sib_off):
        copy.wait_recv()

    weights = cwg[...].reshape(2304, 256)
    lane, sub = iota((8, 256), 1), iota((8, 256), 0)
    for h in range(2):
        pieces = []
        for a in range(3):
            for b in range(3):
                rp, i0 = (0, 0) if a == 1 else (1, a // 2)
                sp, m0 = (0, 0) if b == 1 else (1, b // 2)
                window = grid_in[rp, i0 + 8 * h : i0 + 8 * h + 8, sp, m0 : m0 + 4]
                pieces.append(window.reshape(256, 256).astype(BF16))
        pre = dot(jnp.concatenate(pieces, axis=1), weights) + bias[...]
        features = jax.nn.gelu(pre).astype(BF16)
        blocks = []
        for p in range(4):
            for i in range(8):
                target = i * 32 + ((p - phase[8 * h + i, 0]) & 3) * 8
                blocks.append(onehot(lane == sub + target))
        order = jnp.concatenate(blocks, axis=0).astype(BF16)
        fs[256 * h : 256 * h + 256, :] = dot(order, features).astype(BF16)
        j, c = iota((32, 256), 0), iota((32, 256), 1)
        pick = onehot(j == 4 * (c & 7) + ((c >> 3) & 3)).astype(BF16)
        flags = dot(tissue[8 * h : 8 * h + 8, :].astype(F32).astype(BF16), pick)
        flags = jnp.where(sub == (lane >> 5), flags, 0.0).astype(BF16)
        flags = dot(jnp.ones((8, 8), BF16), flags).astype(BF16)
        fs[512 + 8 * h : 520 + 8 * h, :] = dot_nt(flags, order).astype(BF16)

    own_z.wait()
    for copy in z_copies:
        copy.wait_recv()
    o, c = iota((96, 128), 0), iota((96, 128), 1)
    pack = onehot((o == 6 * (c >> 3) + (c & 7)) & ((c & 7) < 6)).astype(BF16)
    wc[...] = dot(pack, wz[...].reshape(128, HALF)).astype(BF16)

    for copy in z_copies + [
        to_right, to_left, on_right, on_left, sib_left, sib_right, sib_on, sib_off,
        top_copy, left_copy, corner_copy,
    ]:
        copy.wait_send()


def conv_call(feat, cw, bias, w8, phase, tissue):
    vmem = pl.BlockSpec(memory_space=pltpu.VMEM)
    return pl.pallas_call(
        conv_kernel,
        out_shape=(
            jax.ShapeDtypeStruct((528, 256), BF16),
            jax.ShapeDtypeStruct((96, HALF), BF16),
        ),
        in_specs=[vmem, vmem, vmem, vmem, pl.BlockSpec(memory_space=pltpu.SMEM), vmem],
        out_specs=(vmem, vmem),
        scratch_shapes=[
            pltpu.VMEM((2, 17, 2, 5, 8, 256), F32),
            pltpu.VMEM((32, 256), BF16),
            pltpu.VMEM((40, 256), BF16),
            pltpu.VMEM((64, 256), BF16),
            pltpu.VMEM((4, 576, 256), BF16),
            pltpu.VMEM((2, 8, HALF), BF16),
            pltpu.VMEM((16, 8, HALF), BF16),
            pltpu.SemaphoreType.DMA((8,)),
            pltpu.SemaphoreType.DMA((8,)),
            pltpu.SemaphoreType.DMA((3,)),
            pltpu.SemaphoreType.DMA((3,)),
            pltpu.SemaphoreType.DMA((16,)),
            pltpu.SemaphoreType.DMA((16,)),
            pltpu.SemaphoreType.DMA,
        ],
        compiler_params=pltpu.CompilerParams(
            collective_id=0, has_side_effects=True, vmem_limit_bytes=VMEM_LIMIT
        ),
        name="conv",
    )(feat, cw, bias, w8, phase, tissue)


def gather_kernel(
    fs, wc, slots, rings,
    r_send, r_recv, l_send, l_recv, s_send, s_recv, u_send, u_recv, d_send, d_recv, own,
):
    row, col = lax.axis_index("row"), lax.axis_index("col")
    core = lax.rem(row, 2)
    place = lax.rem(row // 2, 4)
    y = row // PLANE
    sibling = (row + 1 - 2 * core, col)
    ahead, behind = (lax.rem(row + 2, ROWS), col), (lax.rem(row + ROWS - 2, ROWS), col)
    above = (lax.rem(row + PLANE, ROWS), col)
    below = (lax.rem(row + ROWS - PLANE, ROWS), col)
    greet([sibling, ahead, behind, above, below])

    def ring(step):
        return lax.rem(y + step + NY, NY)

    own_f = pltpu.make_async_copy(fs, slots.at[0, 0], own.at[0])
    own_w = pltpu.make_async_copy(wc, rings.at[ring(0)], own.at[1])
    own_f.start()
    own_w.start()

    def f_right(t):
        src = fs if t == 0 else slots.at[4 - t, 0]
        return remote(src, slots.at[3 - t, 0], r_send.at[t], r_recv.at[t], ahead)

    def f_left(t):
        src = fs if t == 0 else slots.at[t, 0]
        return remote(src, slots.at[t + 1, 0], l_send.at[t], l_recv.at[t], behind)

    def f_sib(slot):
        src = fs if slot == 0 else slots.at[slot, 0]
        return remote(src, slots.at[slot, 1], s_send.at[slot], s_recv.at[slot], sibling)

    def w_up(t):
        slot = ring(-t)
        src = wc if t == 0 else rings.at[slot]
        dst = rings.at[slot]
        if t == 3:
            src, dst = rings.at[slot, 0:48], rings.at[slot, 0:48]
        return remote(src, dst, u_send.at[t], u_recv.at[t], above)

    def w_down(t):
        slot = ring(t)
        src = wc if t == 0 else rings.at[slot]
        dst = rings.at[slot]
        if t == 3:
            src, dst = rings.at[slot, 48:96], rings.at[slot, 48:96]
        return remote(src, dst, d_send.at[t], d_recv.at[t], below)

    @pl.when(place < 3)
    def _():
        f_right(0).start()

    @pl.when(place > 0)
    def _():
        f_left(0).start()

    w_up(0).start()
    w_down(0).start()
    f_sib(0).start()

    for t in range(1, 4):
        w_up(t - 1).wait_recv()
        w_up(t).start()
        w_down(t - 1).wait_recv()
        w_down(t).start()

        @pl.when(place >= t)
        def _():
            f_right(t - 1).wait_recv()
            f_sib(4 - t).start()

        if t < 3:

            @pl.when((place >= t) & (place < 3))
            def _():
                f_right(t).start()

        @pl.when(3 - place >= t)
        def _():
            f_left(t - 1).wait_recv()
            f_sib(t).start()

        if t < 3:

            @pl.when((3 - place >= t) & (place > 0))
            def _():
                f_left(t).start()

    w_up(3).wait_recv()
    w_down(3).wait_recv()
    own_f.wait()
    own_w.wait()
    for slot in range(4):
        f_sib(slot).wait_recv()
        f_sib(slot).wait_send()
    for t in range(4):
        w_up(t).wait_send()
        w_down(t).wait_send()
    for t in range(3):

        @pl.when((place >= t) & (place < 3))
        def _():
            f_right(t).wait_send()

        @pl.when((3 - place >= t) & (place > 0))
        def _():
            f_left(t).wait_send()


def gather_call(fs, wc):
    vmem = pl.BlockSpec(memory_space=pltpu.VMEM)
    return pl.pallas_call(
        gather_kernel,
        out_shape=(
            jax.ShapeDtypeStruct((4, 2, 528, 256), BF16),
            jax.ShapeDtypeStruct((NY, 96, HALF), BF16),
        ),
        in_specs=[vmem, vmem],
        out_specs=(vmem, vmem),
        scratch_shapes=[pltpu.SemaphoreType.DMA((4,))] * 10 + [pltpu.SemaphoreType.DMA((2,))],
        compiler_params=pltpu.CompilerParams(
            collective_id=1, has_side_effects=True, vmem_limit_bytes=VMEM_LIMIT
        ),
        name="gather",
    )(fs, wc)


def attend_kernel(slots, rings, proj, out, fold, gram, keys, values, dead, queries):
    w = rings[...].reshape(768, HALF)
    p32 = proj[...].astype(F32)
    mean_col = jnp.mean(p32, axis=1, keepdims=True)
    mean_row = dot_nt(jnp.ones((8, 768), BF16), proj[...])[0:1] * (1.0 / 768.0)
    col_sum = dot(jnp.ones((8, 768), BF16), w)[0:1]
    scale = jnp.where(iota((1, HALF), 1) < 384, 0.125 * 1.4426950408889634, 1.0)
    fold[...] = ((dot(proj[...], w) - mean_col * col_sum) * scale).astype(BF16)
    gram[...] = (dot_nt(proj[...], proj[...]) * (1.0 / 768.0) - mean_col * mean_row).astype(BF16)

    lane128 = iota((256, 128), 1)
    first_row = onehot((iota((8, 128), 0) == 0) & (iota((8, 128), 1) == 0)).astype(BF16)
    for q in range(4):
        for c in range(2):
            x = slots[q, c, 0:512, :]
            y = dot(x, gram[...])
            var = jnp.sum(y * x.astype(F32), axis=1, keepdims=True)
            rstd = lax.rsqrt(jnp.maximum(var, 0.0) + 1e-05)
            kv = (dot(x, fold[:, 384:]) * rstd).astype(BF16).reshape(2, 4, 64, 768)
            chunk = 4 * q + 2 * c
            for h in range(2):
                keys[:, chunk + h] = kv[h, :, :, 0:384]
                values[:, chunk + h] = kv[h, :, :, 384:768]
                live = dot_tn(slots[q, c, 512 + 8 * h : 520 + 8 * h, :], first_row)
                bias = jnp.where(lane128 == 0, (live - 1.0) * 1e30, 0.0)
                dead[:, chunk + h] = bias.astype(BF16).reshape(4, 64, 128)
            if q == 0:
                qs = (dot(x, fold[:, 0:384]) * rstd).astype(BF16).reshape(2, 4, 64, 384)
                for h in range(2):
                    queries[:, 2 * c + h] = qs[h]

    lane = iota((256, 128), 1)
    unit = onehot(lane == 0).astype(BF16)
    ones = jnp.ones((1024, 128), BF16)

    def one_phase(p, carry):
        k_all = keys[p].reshape(1024, 384)
        v_all = values[p].reshape(1024, 384)
        q_all = queries[p].reshape(256, 384)
        mask = dead[p].reshape(1024, 128)
        for n in range(3):
            cut = slice(128 * n, 128 * n + 128)
            k_pair = jnp.concatenate([k_all[:, cut], mask], axis=1)
            v_pair = jnp.concatenate([v_all[:, cut], ones], axis=1)
            q_pair = q_all[:, cut].astype(F32)
            both = []
            for e in range(2):
                q_head = jnp.where((lane >= 64) == (e == 1), q_pair, 0.0).astype(BF16)
                scores = dot_nt(jnp.concatenate([q_head, unit], axis=1), k_pair)
                top = jnp.max(scores, axis=1, keepdims=True)
                weights = jnp.exp2(scores - top).astype(BF16)
                mixed = dot(weights, v_pair)
                both.append(mixed[:, 0:128] / mixed[:, 128:256])
            pair = jnp.where(lane < 64, both[0], both[1]).astype(BF16)
            out[p, :, cut] = pair
        return carry

    lax.fori_loop(0, 4, one_phase, 0)


def attend_call(slots, rings, proj):
    vmem = pl.BlockSpec(memory_space=pltpu.VMEM)
    return pl.pallas_call(
        attend_kernel,
        out_shape=jax.ShapeDtypeStruct((4, 256, 384), BF16),
        in_specs=[vmem] * 3,
        out_specs=vmem,
        scratch_shapes=[
            pltpu.VMEM((256, HALF), BF16),
            pltpu.VMEM((256, 256), BF16),
            pltpu.VMEM((4, 16, 64, 384), BF16),
            pltpu.VMEM((4, 16, 64, 384), BF16),
            pltpu.VMEM((4, 16, 64, 128), BF16),
            pltpu.VMEM((4, 4, 64, 384), BF16),
        ],
        compiler_params=pltpu.CompilerParams(vmem_limit_bytes=VMEM_LIMIT),
        name="attend",
    )(slots, rings, proj)


def order_kernel(mixed, flags, phase, out, theirs, send_sem, recv_sem):
    row, col = lax.axis_index("row"), lax.axis_index("col")
    core = lax.rem(row, 2)
    sibling = (row + 1 - 2 * core, col)
    greet([sibling])
    copy = remote(mixed.at[:, 128:256], theirs, send_sem, recv_sem, sibling)
    copy.start()
    orders = []
    j, lane = iota((32, 256), 0), iota((32, 256), 1)
    for h in range(2):
        blocks = []
        for i in range(8):
            p = ((j & 3) + phase[8 * h + i, 0]) & 3
            blocks.append(onehot(lane == p * 64 + i * 8 + (j >> 2)))
        live = flags[8 * h : 8 * h + 1, :].astype(F32)
        orders.append((jnp.concatenate(blocks, axis=0) * live).astype(BF16))
    copy.wait_recv()
    for h in range(2):
        a = mixed[:, 64 * h : 64 * h + 64].reshape(256, 384)
        b = theirs[:, 64 * h : 64 * h + 64].reshape(256, 384)
        a, b = dot(orders[h], a), dot(orders[h], b)
        lower = jnp.where(core == 0, a, b).astype(BF16).reshape(8, 32, 384)
        upper = jnp.where(core == 0, b, a).astype(BF16).reshape(8, 32, 384)
        out[8 * h : 8 * h + 8, :, 0:384] = lower
        out[8 * h : 8 * h + 8, :, 384:768] = upper
    copy.wait_send()


def order_call(mixed, flags, phase):
    vmem = pl.BlockSpec(memory_space=pltpu.VMEM)
    return pl.pallas_call(
        order_kernel,
        out_shape=jax.ShapeDtypeStruct((16, 32, 768), BF16),
        in_specs=[vmem, vmem, pl.BlockSpec(memory_space=pltpu.SMEM)],
        out_specs=vmem,
        scratch_shapes=[
            pltpu.VMEM((4, 128, 384), BF16),
            pltpu.SemaphoreType.DMA,
            pltpu.SemaphoreType.DMA,
        ],
        compiler_params=pltpu.CompilerParams(
            collective_id=2, has_side_effects=True, vmem_limit_bytes=VMEM_LIMIT
        ),
        name="order",
    )(mixed, flags, phase)


def local(feat_in, conv_weight, conv_bias, proj_weight, qkv_weight, tissue, phase):
    w8 = jnp.pad(qkv_weight, ((0, 2), (0, 0)))
    fs, wc = conv_call(feat_in, conv_weight, conv_bias.reshape(1, 256), w8, phase, tissue)
    slots, rings = gather_call(fs, wc)
    mixed = attend_call(slots, rings, proj_weight)
    return order_call(mixed, fs[512:528], phase)


def solution(mesh):
    in_specs = (
        P("row", "col", None),
        P("col", None),
        P(),
        P(),
        P("row", None),
        P("row", "col"),
        P("row", "col"),
    )
    out_specs = P("row", "col", None)
    return jax.shard_map(local, mesh=mesh, in_specs=in_specs, out_specs=out_specs, check_vma=False)
```

```python
import jax
import jax.numpy as jnp
from jax import lax
from jax.experimental import pallas as pl
from jax.experimental.pallas import tpu as pltpu
from jax.sharding import PartitionSpec as P

MESH = pl.DeviceIdType.MESH
F32 = jnp.float32
BF16 = jnp.bfloat16
ROWS = 128
COLS = 4
PLANE = 16
NY = 8
HALF = 1152
VMEM_LIMIT = 56 * 1024 * 1024


def iota(shape, dim):
    return lax.broadcasted_iota(jnp.int32, shape, dim)


def onehot(cond):
    return jnp.where(cond, 1.0, 0.0)


def dot(a, b):
    return jnp.dot(a, b, preferred_element_type=F32)


def dot_nt(a, b):
    return lax.dot_general(a, b, (((1,), (1,)), ((), ())), preferred_element_type=F32)


def dot_tn(a, b):
    return lax.dot_general(a, b, (((0,), (0,)), ((), ())), preferred_element_type=F32)


def remote(src, dst, send_sem, recv_sem, device):
    return pltpu.make_async_remote_copy(
        src_ref=src,
        dst_ref=dst,
        send_sem=send_sem,
        recv_sem=recv_sem,
        device_id=device,
        device_id_type=MESH,
    )


def greet(devices):
    barrier = pltpu.get_barrier_semaphore()
    for device in devices:
        pl.semaphore_signal(barrier, inc=1, device_id=device, device_id_type=MESH)
    pl.semaphore_wait(barrier, len(devices))


def whole_kernel(
    feat, cw, bias, w6, proj, phase, tissue, out,
    grid_in, ext, halo, top, cwg, wsend, wz, rings, slots, flags, orders,
    fold, gram, keys, values, dead, queries, mixed, theirs,
    cw_send, cw_recv, h_send, h_recv, z_send, z_recv, g_send, g_recv,
    f_send, f_recv, s_send, s_recv, u_send, u_recv, d_send, d_recv, m_send, m_recv, own_sem,
):
    row, col = lax.axis_index("row"), lax.axis_index("col")
    core = lax.rem(row, 2)
    base = row - lax.rem(row, PLANE)
    mine = row - base
    y_at = row // PLANE
    place = lax.rem(row // 2, 4)
    sibling = (row + 1 - 2 * core, col)
    right, left = lax.rem(col + 1, COLS), lax.rem(col + COLS - 1, COLS)
    across = lax.rem(col + 2, COLS)
    down, up = lax.rem(row + 1, ROWS), lax.rem(row + ROWS - 1, ROWS)
    above = (lax.rem(row + PLANE, ROWS), col)
    below = (lax.rem(row + ROWS - PLANE, ROWS), col)
    plane = [(base + lax.rem(mine + k, PLANE), col) for k in range(1, PLANE)]
    greet(
        [(row, right), (row, left), (down, col), (up, col), (down, right), (up, left)]
        + [above, below]
        + plane
    )

    part = pl.multiple_of(core * 288, 32)

    def cw_piece(slot, start, size):
        return cwg.at[slot, pl.ds(pl.multiple_of(part + start, 16), size), :]

    def cw_copy(i, slot, start, size, device):
        piece = cw_piece(slot, start, size)
        return remote(piece, piece, cw_send.at[i], cw_recv.at[i], device)

    own_cw = pltpu.make_async_copy(cw, cwg.at[col], own_sem.at[0])
    own_cw.start()
    half = cw.at[pl.ds(part, 288), :]
    to_right = remote(half, cw_piece(col, 0, 288), cw_send.at[0], cw_recv.at[0], (row, right))
    to_left = remote(half, cw_piece(col, 0, 288), cw_send.at[1], cw_recv.at[1], (row, left))
    to_right.start()
    to_left.start()
    top_copy = remote(feat.at[31], top, h_send.at[0], h_recv.at[0], (down, col))
    top_copy.start()

    for c in range(2):
        wsend[c] = jnp.zeros((8, HALF), BF16)
        for j in range(3):
            wsend[c, 0:6, 384 * j : 384 * j + 384] = w6[
                :, 768 * j + 384 * c : 768 * j + 384 * c + 384
            ]
    z_copies = []
    for k in range(1, PLANE):
        to_core = lax.rem(core + k, 2)
        copy = remote(
            wsend.at[to_core], wz.at[mine], z_send.at[k], z_recv.at[k], plane[k - 1]
        )
        copy.start()
        z_copies.append(copy)
    own_z = pltpu.make_async_copy(wsend.at[core], wz.at[mine], own_sem.at[1])
    own_z.start()

    o, c = iota((256, 256), 0), iota((256, 256), 1)
    k, si, sp = o & 7, (o >> 3) & 3, (o >> 5) & 1
    r = 2 * ((o >> 6) & 1) + (o >> 7)
    split = onehot(c == r * 64 + 8 * k + 2 * si + sp).astype(BF16)
    for g in range(8):
        x = feat[4 * g : 4 * g + 4].reshape(256, 256)
        y = dot(split, x).reshape(2, 2, 2, 4, 8, 256)
        grid_in[0, 2 * g : 2 * g + 2, 0, 0:4] = y[0, :, 0]
        grid_in[0, 2 * g : 2 * g + 2, 1, 1:5] = y[0, :, 1]
        grid_in[1, 2 * g + 1 : 2 * g + 3, 0, 0:4] = y[1, :, 0]
        grid_in[1, 2 * g + 1 : 2 * g + 3, 1, 1:5] = y[1, :, 1]

    for rp in range(2):
        for i in range(0, 16, 8):
            rows8 = [grid_in[rp, rp + i + e, 1, 4, 7:8, :] for e in range(8)]
            ext[16 * rp + i : 16 * rp + i + 8, :] = jnp.concatenate(rows8, axis=0).astype(BF16)
    left_copy = remote(ext, halo.at[0:32], h_send.at[1], h_recv.at[1], (row, right))
    left_copy.start()
    corner_copy = remote(
        ext.at[24:32], halo.at[32:40], h_send.at[2], h_recv.at[2], (down, right)
    )
    corner_copy.start()

    lane, sub = iota((8, 256), 1), iota((8, 256), 0)
    for h in range(2):
        blocks = []
        for p in range(4):
            for i in range(8):
                target = i * 32 + ((p - phase[8 * h + i, 0]) & 3) * 8
                blocks.append(onehot(lane == sub + target))
        order = jnp.concatenate(blocks, axis=0).astype(BF16)
        orders[h] = order
        j, c = iota((32, 256), 0), iota((32, 256), 1)
        pick = onehot(j == 4 * (c & 7) + ((c >> 3) & 3)).astype(BF16)
        live = dot(tissue[8 * h : 8 * h + 8, :].astype(F32).astype(BF16), pick)
        live = jnp.where(sub == (lane >> 5), live, 0.0).astype(BF16)
        live = dot(jnp.ones((8, 8), BF16), live).astype(BF16)
        flags[0, 0, :, 256 * h : 256 * h + 256] = dot_nt(live, order).astype(BF16)
    g_copies = []
    for dz in range(4):
        for dc in range(2):
            if dz or dc:
                n = 2 * dz + dc
                peer = row + 2 * (lax.rem(place + dz, 4) - place) + dc * (1 - 2 * core)
                copy = remote(
                    flags.at[0, 0], flags.at[(4 - dz) % 4, dc], g_send.at[n], g_recv.at[n], (peer, col)
                )
                copy.start()
                g_copies.append(copy)

    to_right.wait_recv()
    on_right = cw_copy(2, left, 0, 144, (row, right))
    on_right.start()
    sib_left = cw_copy(4, left, 0, 288, sibling)
    sib_left.start()
    to_left.wait_recv()
    on_left = cw_copy(3, right, 144, 144, (row, left))
    on_left.start()
    sib_right = cw_copy(5, right, 0, 288, sibling)
    sib_right.start()

    own_z.wait()
    for copy in z_copies:
        copy.wait_recv()
    o, c = iota((96, 128), 0), iota((96, 128), 1)
    pack = onehot((o == 6 * (c >> 3) + (c & 7)) & ((c & 7) < 6)).astype(BF16)
    rings[y_at] = dot(pack, wz[...].reshape(128, HALF)).astype(BF16)

    def w_up(t):
        piece = rings.at[lax.rem(y_at + NY - t, NY)]
        piece = piece.at[0:48] if t == 3 else piece
        return remote(piece, piece, u_send.at[t], u_recv.at[t], above)

    def w_down(t):
        piece = rings.at[lax.rem(y_at + t, NY)]
        piece = piece.at[48:96] if t == 3 else piece
        return remote(piece, piece, d_send.at[t], d_recv.at[t], below)

    w_up(0).start()
    w_down(0).start()

    top_copy.wait_recv()
    left_copy.wait_recv()
    corner_copy.wait_recv()
    inside = row > 0
    inner = col > 0
    o, c = iota((64, 64), 0), iota((64, 64), 1)
    split_row = onehot(c == 8 * (o & 7) + 2 * ((o >> 3) & 3) + (o >> 5)).astype(BF16)
    yt = jnp.where(inside, dot(split_row, top[...]), 0.0).reshape(2, 4, 8, 256)
    grid_in[1, 0, 0, 0:4] = yt[0]
    grid_in[1, 0, 1, 1:5] = yt[1]
    o, c = iota((264, 40), 0), iota((264, 40), 1)
    source = o >> 3
    source = jnp.where(source < 16, source, jnp.where(source == 16, 39, source - 1))
    spread = onehot((c == source) & ((o & 7) == 0)).astype(BF16)
    edge = jnp.where(inner, dot(spread, halo[...]), 0.0).reshape(33, 8, 256)
    first = iota((1, 8, 256), 1) == 0
    moved = pltpu.roll(grid_in[0, 0:16, 1, 4], 1, 1)
    grid_in[0, 0:16, 1, 0] = jnp.where(first, edge[0:16], moved)
    moved = pltpu.roll(grid_in[1, 0:17, 1, 4], 1, 1)
    keep = edge[16:33]
    keep = jnp.where((iota((17, 8, 256), 0) == 0) & jnp.logical_not(inside), 0.0, keep)
    grid_in[1, 0:17, 1, 0] = jnp.where(first, keep, moved)

    on_right.wait_recv()
    sib_on = cw_copy(6, across, 0, 144, sibling)
    sib_on.start()
    on_left.wait_recv()
    sib_off = cw_copy(7, across, 144, 144, sibling)
    sib_off.start()
    own_cw.wait()
    for copy in (sib_left, sib_right, sib_on, sib_off):
        copy.wait_recv()

    weights = cwg[...].reshape(2304, 256)
    for h in range(2):
        pieces = []
        for a in range(3):
            for b in range(3):
                rp, i0 = (0, 0) if a == 1 else (1, a // 2)
                sp, m0 = (0, 0) if b == 1 else (1, b // 2)
                window = grid_in[rp, i0 + 8 * h : i0 + 8 * h + 8, sp, m0 : m0 + 4]
                pieces.append(window.reshape(256, 256).astype(BF16))
        pre = dot(jnp.concatenate(pieces, axis=1), weights) + bias[...]
        features = jax.nn.gelu(pre).astype(BF16)
        placed = dot(orders[h], features).astype(BF16).reshape(4, 64, 256)
        slots[0, 0, :, 64 * h : 64 * h + 64, :] = placed

    def f_right(p):
        return remote(
            slots.at[0, 0, p], slots.at[3, 0, p], f_send.at[0, p], f_recv.at[3, p],
            (lax.rem(row + 2, ROWS), col),
        )

    def f_left(p):
        return remote(
            slots.at[0, 0, p], slots.at[1, 0, p], f_send.at[1, p], f_recv.at[1, p],
            (lax.rem(row + ROWS - 2, ROWS), col),
        )

    def f_two(p):
        return remote(
            slots.at[0, 0, p], slots.at[2, 0, p], f_send.at[2, p], f_recv.at[2, p],
            (row + 4 * jnp.where(place < 2, 1, -1), col),
        )

    def f_far(p):
        to = jnp.where(place == 2, 1, 3)
        return remote(
            slots.at[2, 0, p], slots.at[to, 0, p], f_send.at[3, p], f_recv.at[to, p],
            (row + 2 * jnp.where(place == 2, 1, -1), col),
        )

    def f_sib(slot, p):
        piece = slots.at[slot, 0, p]
        return remote(piece, slots.at[slot, 1, p], s_send.at[slot, p], s_recv.at[slot, p], sibling)

    def arrived(slot, p):
        piece = slots.at[slot, 0, p]
        return remote(piece, piece, f_send.at[0, p], f_recv.at[slot, p], sibling)

    for p in range(4):

        @pl.when(place < 3)
        def _():
            f_right(p).start()

        @pl.when(place > 0)
        def _():
            f_left(p).start()

        f_two(p).start()
        f_sib(0, p).start()

    def serve(p):
        arrived(2, p).wait_recv()

        @pl.when((place == 1) | (place == 2))
        def _():
            f_far(p).start()

        f_sib(2, p).start()
        for slot in (1, 3):
            arrived(slot, p).wait_recv()
            f_sib(slot, p).start()

    p32 = proj[...].astype(F32)
    mean_col = jnp.mean(p32, axis=1, keepdims=True)
    mean_row = dot_nt(jnp.ones((8, 768), BF16), proj[...])[0:1] * (1.0 / 768.0)
    gram[...] = (dot_nt(proj[...], proj[...]) * (1.0 / 768.0) - mean_col * mean_row).astype(BF16)
    for copy in g_copies:
        copy.wait_recv()
    lane128 = iota((512, 128), 1)
    first_row = onehot((iota((8, 128), 0) == 0) & (iota((8, 128), 1) == 0)).astype(BF16)
    for q in range(4):
        for c in range(2):
            live = dot_tn(flags[q, c], first_row)
            gone = jnp.where((lane128 == 0) , (live - 1.0) * 1e30, 0.0).astype(BF16)
            gone = gone.reshape(2, 4, 64, 128)
            for h in range(2):
                dead[:, q, c, 64 * h : 64 * h + 64, :] = gone[h]

    w_up(0).wait_recv()
    w_up(1).start()
    w_down(0).wait_recv()
    w_down(1).start()
    serve(0)
    w_up(1).wait_recv()
    w_up(2).start()
    w_down(1).wait_recv()
    w_down(2).start()
    serve(1)
    w_up(2).wait_recv()
    w_up(3).start()
    w_down(2).wait_recv()
    w_down(3).start()
    w_up(3).wait_recv()
    w_down(3).wait_recv()

    w = rings[...].reshape(768, HALF)
    col_sum = dot(jnp.ones((8, 768), BF16), w)[0:1]
    scale = jnp.where(iota((1, HALF), 1) < 384, 0.125 * 1.4426950408889634, 1.0)
    fold[...] = ((dot(proj[...], w) - mean_col * col_sum) * scale).astype(BF16)

    lane = iota((256, 128), 1)
    unit = onehot(lane == 0).astype(BF16)
    ones = jnp.ones((1024, 128), BF16)

    def give(p):
        return remote(mixed.at[p, 128:256], theirs.at[p], m_send.at[p], m_recv.at[p], sibling)

    def one_phase(p, carry):
        for slot in range(4):
            f_sib(slot, p).wait_recv()
        x = slots[:, :, p].reshape(1024, 256)
        y = dot(x, gram[...])
        var = jnp.sum(y * x.astype(F32), axis=1, keepdims=True)
        rstd = lax.rsqrt(jnp.maximum(var, 0.0) + 1e-05)
        kv = (dot(x, fold[:, 384:]) * rstd).astype(BF16)
        keys[...] = kv[:, 0:384]
        values[...] = kv[:, 384:768]
        queries[...] = (dot(x[0:256], fold[:, 0:384]) * rstd[0:256]).astype(BF16)
        mask = dead[p].reshape(1024, 128)
        for n in range(3):
            if n == 1:

                @pl.when(p < 2)
                def _():
                    serve(p + 2)

            cut = slice(128 * n, 128 * n + 128)
            k_pair = jnp.concatenate([keys[:, cut], mask], axis=1)
            v_pair = jnp.concatenate([values[:, cut], ones], axis=1)
            q_pair = queries[:, cut].astype(F32)
            both = []
            for e in range(2):
                q_head = jnp.where((lane >= 64) == (e == 1), q_pair, 0.0).astype(BF16)
                scores = dot_nt(jnp.concatenate([q_head, unit], axis=1), k_pair)
                highest = jnp.max(scores, axis=1, keepdims=True)
                weights = jnp.exp2(scores - highest).astype(BF16)
                result = dot(weights, v_pair)
                both.append(result[:, 0:128] / result[:, 128:256])
            mixed[p, :, cut] = jnp.where(lane < 64, both[0], both[1]).astype(BF16)
        give(p).start()
        return carry

    lax.fori_loop(0, 4, one_phase, 0)

    back = []
    j, lane = iota((32, 256), 0), iota((32, 256), 1)
    for h in range(2):
        blocks = []
        for i in range(8):
            p = ((j & 3) + phase[8 * h + i, 0]) & 3
            blocks.append(onehot(lane == p * 64 + i * 8 + (j >> 2)))
        live = flags[0, 0, 0:1, 256 * h : 256 * h + 256].astype(F32)
        back.append((jnp.concatenate(blocks, axis=0) * live).astype(BF16))
    for p in range(4):
        give(p).wait_recv()
    for h in range(2):
        a = mixed[:, 64 * h : 64 * h + 64].reshape(256, 384)
        b = theirs[:, 64 * h : 64 * h + 64].reshape(256, 384)
        a, b = dot(back[h], a), dot(back[h], b)
        lower = jnp.where(core == 0, a, b).astype(BF16).reshape(8, 32, 384)
        upper = jnp.where(core == 0, b, a).astype(BF16).reshape(8, 32, 384)
        out[8 * h : 8 * h + 8, :, 0:384] = lower
        out[8 * h : 8 * h + 8, :, 384:768] = upper

    for copy in z_copies + g_copies + [
        to_right, to_left, on_right, on_left, sib_left, sib_right, sib_on, sib_off,
        top_copy, left_copy, corner_copy,
    ]:
        copy.wait_send()
    for t in range(4):
        w_up(t).wait_send()
        w_down(t).wait_send()
    for p in range(4):
        give(p).wait_send()
        f_two(p).wait_send()
        for slot in range(4):
            f_sib(slot, p).wait_send()

        @pl.when(place < 3)
        def _():
            f_right(p).wait_send()

        @pl.when(place > 0)
        def _():
            f_left(p).wait_send()

        @pl.when((place == 1) | (place == 2))
        def _():
            f_far(p).wait_send()


def local(feat_in, conv_weight, conv_bias, proj_weight, qkv_weight, tissue, phase):
    vmem = pl.BlockSpec(memory_space=pltpu.VMEM)
    dma = pltpu.SemaphoreType.DMA
    return pl.pallas_call(
        whole_kernel,
        out_shape=jax.ShapeDtypeStruct((16, 32, 768), BF16),
        in_specs=[vmem] * 5 + [pl.BlockSpec(memory_space=pltpu.SMEM), vmem],
        out_specs=vmem,
        scratch_shapes=[
            pltpu.VMEM((2, 17, 2, 5, 8, 256), F32),
            pltpu.VMEM((32, 256), BF16),
            pltpu.VMEM((40, 256), BF16),
            pltpu.VMEM((64, 256), BF16),
            pltpu.VMEM((4, 576, 256), BF16),
            pltpu.VMEM((2, 8, HALF), BF16),
            pltpu.VMEM((16, 8, HALF), BF16),
            pltpu.VMEM((NY, 96, HALF), BF16),
            pltpu.VMEM((4, 2, 4, 128, 256), BF16),
            pltpu.VMEM((4, 2, 8, 512), BF16),
            pltpu.VMEM((2, 256, 256), BF16),
            pltpu.VMEM((256, HALF), BF16),
            pltpu.VMEM((256, 256), BF16),
            pltpu.VMEM((1024, 384), BF16),
            pltpu.VMEM((1024, 384), BF16),
            pltpu.VMEM((4, 4, 2, 128, 128), BF16),
            pltpu.VMEM((256, 384), BF16),
            pltpu.VMEM((4, 256, 384), BF16),
            pltpu.VMEM((4, 128, 384), BF16),
            dma((8,)), dma((8,)),
            dma((3,)), dma((3,)),
            dma((16,)), dma((16,)),
            dma((8,)), dma((8,)),
            dma((4, 4)), dma((4, 4)),
            dma((4, 4)), dma((4, 4)),
            dma((4,)), dma((4,)),
            dma((4,)), dma((4,)),
            dma((4,)), dma((4,)),
            dma((2,)),
        ],
        compiler_params=pltpu.CompilerParams(
            collective_id=0, has_side_effects=True, vmem_limit_bytes=VMEM_LIMIT
        ),
        name="whole",
    )(
        feat_in, conv_weight, conv_bias.reshape(1, 256), qkv_weight, proj_weight, phase, tissue
    )


def solution(mesh):
    in_specs = (
        P("row", "col", None),
        P("col", None),
        P(),
        P(),
        P("row", None),
        P("row", "col"),
        P("row", "col"),
    )
    out_specs = P("row", "col", None)
    return jax.shard_map(local, mesh=mesh, in_specs=in_specs, out_specs=out_specs, check_vma=False)
```

```python
import jax
import jax.numpy as jnp
from jax import lax
from jax.experimental import pallas as pl
from jax.experimental.pallas import tpu as pltpu
from jax.sharding import PartitionSpec as P

MESH = pl.DeviceIdType.MESH
F32 = jnp.float32
BF16 = jnp.bfloat16
ROWS = 128
COLS = 4
PLANE = 16
NY = 8
HALF = 1152
PART = 640
REST = HALF - PART
VMEM_LIMIT = 56 * 1024 * 1024


def iota(shape, dim):
    return lax.broadcasted_iota(jnp.int32, shape, dim)


def onehot(cond):
    return jnp.where(cond, 1.0, 0.0)


def dot(a, b):
    return jnp.dot(a, b, preferred_element_type=F32)


def dot_nt(a, b):
    return lax.dot_general(a, b, (((1,), (1,)), ((), ())), preferred_element_type=F32)


def dot_tn(a, b):
    return lax.dot_general(a, b, (((0,), (0,)), ((), ())), preferred_element_type=F32)


def remote(src, dst, send_sem, recv_sem, device):
    return pltpu.make_async_remote_copy(
        src_ref=src,
        dst_ref=dst,
        send_sem=send_sem,
        recv_sem=recv_sem,
        device_id=device,
        device_id_type=MESH,
    )


def greet(devices):
    barrier = pltpu.get_barrier_semaphore()
    for device in devices:
        pl.semaphore_signal(barrier, inc=1, device_id=device, device_id_type=MESH)
    pl.semaphore_wait(barrier, len(devices))


def whole_kernel(
    feat, cw, bias, w6, proj, phase, tissue, out,
    grid_in, ext, halo, top, cwg, wsend, wz, rings, wsend_b, wz_b, rings_b, proj_b, slots, flags, orders,
    fold, gram, keys, values, dead, queries, mixed, theirs,
    cw_send, cw_recv, h_send, h_recv, z_send, z_recv, g_send, g_recv,
    f_send, f_recv, s_send, s_recv, zb_send, zb_recv, u_send, u_recv, m_send, m_recv, own_sem,
):
    row, col = lax.axis_index("row"), lax.axis_index("col")
    core = lax.rem(row, 2)
    base = row - lax.rem(row, PLANE)
    mine = row - base
    y_at = row // PLANE
    place = lax.rem(row // 2, 4)
    sibling = (row + 1 - 2 * core, col)
    right, left = lax.rem(col + 1, COLS), lax.rem(col + COLS - 1, COLS)
    across = lax.rem(col + 2, COLS)
    down, up = lax.rem(row + 1, ROWS), lax.rem(row + ROWS - 1, ROWS)
    above = (lax.rem(row + PLANE, ROWS), col)
    below = (lax.rem(row + ROWS - PLANE, ROWS), col)
    plane = [(base + lax.rem(mine + k, PLANE), col) for k in range(1, PLANE)]
    z_at = mine // 2
    pole_at = 2 * y_at + core
    pole = []
    for k in range(1, PLANE):
        other = lax.rem(pole_at + k, PLANE)
        pole.append((PLANE * (other // 2) + 2 * z_at + lax.rem(other, 2), col))
    ahead = (base + lax.rem(mine + 2, PLANE), col)
    behind = (base + lax.rem(mine + PLANE - 2, PLANE), col)
    greet(
        [(row, right), (row, left), (down, col), (up, col), (down, right), (up, left)]
        + plane
        + pole
    )

    part = pl.multiple_of(core * 288, 32)

    def cw_piece(slot, start, size):
        return cwg.at[slot, pl.ds(pl.multiple_of(part + start, 16), size), :]

    def cw_copy(i, slot, start, size, device):
        piece = cw_piece(slot, start, size)
        return remote(piece, piece, cw_send.at[i], cw_recv.at[i], device)

    own_cw = pltpu.make_async_copy(cw, cwg.at[col], own_sem.at[0])
    own_cw.start()
    half = cw.at[pl.ds(part, 288), :]
    to_right = remote(half, cw_piece(col, 0, 288), cw_send.at[0], cw_recv.at[0], (row, right))
    to_left = remote(half, cw_piece(col, 0, 288), cw_send.at[1], cw_recv.at[1], (row, left))
    to_right.start()
    to_left.start()
    top_copy = remote(feat.at[31], top, h_send.at[0], h_recv.at[0], (down, col))
    top_copy.start()

    for c in range(2):
        wsend[c] = jnp.zeros((8, PART), BF16)
        wsend_b[c] = jnp.zeros((8, REST), BF16)
        for n in range(9):
            at = 768 * (n // 3) + 384 * c + 128 * (n % 3)
            block = w6[:, at : at + 128]
            if n < 5:
                wsend[c, 0:6, 128 * n : 128 * n + 128] = block
            else:
                wsend_b[c, 0:6, 128 * n - PART : 128 * n + 128 - PART] = block
    z_copies = []
    for k in range(1, PLANE):
        to_core = lax.rem(core + k, 2)
        copy = remote(
            wsend.at[to_core], wz.at[mine], z_send.at[k], z_recv.at[k], plane[k - 1]
        )
        copy.start()
        z_copies.append(copy)
        copy = remote(
            wsend_b.at[to_core], wz_b.at[pole_at], zb_send.at[k], zb_recv.at[k], pole[k - 1]
        )
        copy.start()
        z_copies.append(copy)
    own_z = pltpu.make_async_copy(wsend.at[core], wz.at[mine], own_sem.at[1])
    own_z.start()
    own_y = pltpu.make_async_copy(wsend_b.at[core], wz_b.at[pole_at], own_sem.at[2])
    own_y.start()

    o, c = iota((256, 256), 0), iota((256, 256), 1)
    k, si, sp = o & 7, (o >> 3) & 3, (o >> 5) & 1
    r = 2 * ((o >> 6) & 1) + (o >> 7)
    split = onehot(c == r * 64 + 8 * k + 2 * si + sp).astype(BF16)
    for g in range(8):
        x = feat[4 * g : 4 * g + 4].reshape(256, 256)
        y = dot(split, x).reshape(2, 2, 2, 4, 8, 256)
        grid_in[0, 2 * g : 2 * g + 2, 0, 0:4] = y[0, :, 0]
        grid_in[0, 2 * g : 2 * g + 2, 1, 1:5] = y[0, :, 1]
        grid_in[1, 2 * g + 1 : 2 * g + 3, 0, 0:4] = y[1, :, 0]
        grid_in[1, 2 * g + 1 : 2 * g + 3, 1, 1:5] = y[1, :, 1]

    for rp in range(2):
        for i in range(0, 16, 8):
            rows8 = [grid_in[rp, rp + i + e, 1, 4, 7:8, :] for e in range(8)]
            ext[16 * rp + i : 16 * rp + i + 8, :] = jnp.concatenate(rows8, axis=0).astype(BF16)
    left_copy = remote(ext, halo.at[0:32], h_send.at[1], h_recv.at[1], (row, right))
    left_copy.start()
    corner_copy = remote(
        ext.at[24:32], halo.at[32:40], h_send.at[2], h_recv.at[2], (down, right)
    )
    corner_copy.start()

    lane, sub = iota((8, 256), 1), iota((8, 256), 0)
    for h in range(2):
        blocks = []
        for p in range(4):
            for i in range(8):
                target = i * 32 + ((p - phase[8 * h + i, 0]) & 3) * 8
                blocks.append(onehot(lane == sub + target))
        order = jnp.concatenate(blocks, axis=0).astype(BF16)
        orders[h] = order
        j, c = iota((32, 256), 0), iota((32, 256), 1)
        pick = onehot(j == 4 * (c & 7) + ((c >> 3) & 3)).astype(BF16)
        live = dot(tissue[8 * h : 8 * h + 8, :].astype(F32).astype(BF16), pick)
        live = jnp.where(sub == (lane >> 5), live, 0.0).astype(BF16)
        live = dot(jnp.ones((8, 8), BF16), live).astype(BF16)
        flags[0, 0, :, 256 * h : 256 * h + 256] = dot_nt(live, order).astype(BF16)
    g_copies = []
    for dz in range(4):
        for dc in range(2):
            if dz or dc:
                n = 2 * dz + dc
                peer = row + 2 * (lax.rem(place + dz, 4) - place) + dc * (1 - 2 * core)
                copy = remote(
                    flags.at[0, 0], flags.at[(4 - dz) % 4, dc], g_send.at[n], g_recv.at[n], (peer, col)
                )
                copy.start()
                g_copies.append(copy)

    to_right.wait_recv()
    on_right = cw_copy(2, left, 0, 144, (row, right))
    on_right.start()
    sib_left = cw_copy(4, left, 0, 288, sibling)
    sib_left.start()
    to_left.wait_recv()
    on_left = cw_copy(3, right, 144, 144, (row, left))
    on_left.start()
    sib_right = cw_copy(5, right, 0, 288, sibling)
    sib_right.start()

    own_z.wait()
    own_y.wait()
    for copy in z_copies:
        copy.wait_recv()
    o, c = iota((96, 128), 0), iota((96, 128), 1)
    pack = onehot((o == 6 * (c >> 3) + (c & 7)) & ((c & 7) < 6)).astype(BF16)
    rings[y_at] = dot(pack, wz[...].reshape(128, PART)).astype(BF16)
    rings_b[z_at] = dot(pack, wz_b[...].reshape(128, REST)).astype(BF16)

    def ring(n, t):
        buffer, at, to = ((rings, y_at, (above, below)), (rings_b, z_at, (ahead, behind)))[n // 2]
        if n % 2 == 0:
            piece = buffer.at[lax.rem(at + NY - t, NY)]
            piece = piece.at[0:48] if t == 3 else piece
        else:
            piece = buffer.at[lax.rem(at + t, NY)]
            piece = piece.at[48:96] if t == 3 else piece
        return remote(piece, piece, u_send.at[n, t], u_recv.at[n, t], to[n % 2])

    def ring_step(t):
        for n in range(4):
            if t > 0:
                ring(n, t - 1).wait_recv()
            if t < 4:
                ring(n, t).start()

    ring_step(0)

    top_copy.wait_recv()
    left_copy.wait_recv()
    corner_copy.wait_recv()
    inside = row > 0
    inner = col > 0
    o, c = iota((64, 64), 0), iota((64, 64), 1)
    split_row = onehot(c == 8 * (o & 7) + 2 * ((o >> 3) & 3) + (o >> 5)).astype(BF16)
    yt = jnp.where(inside, dot(split_row, top[...]), 0.0).reshape(2, 4, 8, 256)
    grid_in[1, 0, 0, 0:4] = yt[0]
    grid_in[1, 0, 1, 1:5] = yt[1]
    o, c = iota((264, 40), 0), iota((264, 40), 1)
    source = o >> 3
    source = jnp.where(source < 16, source, jnp.where(source == 16, 39, source - 1))
    spread = onehot((c == source) & ((o & 7) == 0)).astype(BF16)
    edge = jnp.where(inner, dot(spread, halo[...]), 0.0).reshape(33, 8, 256)
    first = iota((1, 8, 256), 1) == 0
    moved = pltpu.roll(grid_in[0, 0:16, 1, 4], 1, 1)
    grid_in[0, 0:16, 1, 0] = jnp.where(first, edge[0:16], moved)
    moved = pltpu.roll(grid_in[1, 0:17, 1, 4], 1, 1)
    keep = edge[16:33]
    keep = jnp.where((iota((17, 8, 256), 0) == 0) & jnp.logical_not(inside), 0.0, keep)
    grid_in[1, 0:17, 1, 0] = jnp.where(first, keep, moved)

    p32 = proj[...].astype(F32)
    mean_col = jnp.mean(p32, axis=1, keepdims=True)
    mean_row = dot_nt(jnp.ones((8, 768), BF16), proj[...])[0:1] * (1.0 / 768.0)
    gram[...] = (dot_nt(proj[...], proj[...]) * (1.0 / 768.0) - mean_col * mean_row).astype(BF16)
    s_at, d_at = iota((768, 768), 0), iota((1, 768), 1)
    big = (d_at * 683) >> 16
    small = ((d_at - 96 * big) * 5462) >> 16
    swapped = 96 * small + 12 * big + d_at - 96 * big - 12 * small
    proj_b[...] = dot(proj[...], onehot(s_at == swapped).astype(BF16)).astype(BF16)

    ring_step(1)

    on_right.wait_recv()
    sib_on = cw_copy(6, across, 0, 144, sibling)
    sib_on.start()
    on_left.wait_recv()
    sib_off = cw_copy(7, across, 144, 144, sibling)
    sib_off.start()
    own_cw.wait()
    for copy in (sib_left, sib_right, sib_on, sib_off):
        copy.wait_recv()

    weights = cwg[...].reshape(2304, 256)
    for h in range(2):
        pieces = []
        for a in range(3):
            for b in range(3):
                rp, i0 = (0, 0) if a == 1 else (1, a // 2)
                sp, m0 = (0, 0) if b == 1 else (1, b // 2)
                window = grid_in[rp, i0 + 8 * h : i0 + 8 * h + 8, sp, m0 : m0 + 4]
                pieces.append(window.reshape(256, 256).astype(BF16))
        pre = dot(jnp.concatenate(pieces, axis=1), weights) + bias[...]
        features = jax.nn.gelu(pre).astype(BF16)
        placed = dot(orders[h], features).astype(BF16).reshape(4, 64, 256)
        slots[0, 0, :, 64 * h : 64 * h + 64, :] = placed

    def f_right(p):
        return remote(
            slots.at[0, 0, p], slots.at[3, 0, p], f_send.at[0, p], f_recv.at[3, p],
            (lax.rem(row + 2, ROWS), col),
        )

    def f_left(p):
        return remote(
            slots.at[0, 0, p], slots.at[1, 0, p], f_send.at[1, p], f_recv.at[1, p],
            (lax.rem(row + ROWS - 2, ROWS), col),
        )

    def f_two(p):
        return remote(
            slots.at[0, 0, p], slots.at[2, 0, p], f_send.at[2, p], f_recv.at[2, p],
            (row + 4 * jnp.where(place < 2, 1, -1), col),
        )

    def f_far(p):
        to = jnp.where(place == 2, 1, 3)
        return remote(
            slots.at[2, 0, p], slots.at[to, 0, p], f_send.at[3, p], f_recv.at[to, p],
            (row + 2 * jnp.where(place == 2, 1, -1), col),
        )

    def f_sib(slot, p):
        piece = slots.at[slot, 0, p]
        return remote(piece, slots.at[slot, 1, p], s_send.at[slot, p], s_recv.at[slot, p], sibling)

    def arrived(slot, p):
        piece = slots.at[slot, 0, p]
        return remote(piece, piece, f_send.at[0, p], f_recv.at[slot, p], sibling)

    for p in range(4):

        @pl.when(place < 3)
        def _():
            f_right(p).start()

        @pl.when(place > 0)
        def _():
            f_left(p).start()

        f_two(p).start()
        f_sib(0, p).start()

    def serve(p):
        arrived(2, p).wait_recv()

        @pl.when((place == 1) | (place == 2))
        def _():
            f_far(p).start()

        f_sib(2, p).start()
        for slot in (1, 3):
            arrived(slot, p).wait_recv()
            f_sib(slot, p).start()

    ring_step(2)
    for copy in g_copies:
        copy.wait_recv()
    lane128 = iota((512, 128), 1)
    first_row = onehot((iota((8, 128), 0) == 0) & (iota((8, 128), 1) == 0)).astype(BF16)
    for q in range(4):
        for c in range(2):
            live = dot_tn(flags[q, c], first_row)
            gone = jnp.where((lane128 == 0) , (live - 1.0) * 1e30, 0.0).astype(BF16)
            gone = gone.reshape(2, 4, 64, 128)
            for h in range(2):
                dead[:, q, c, 64 * h : 64 * h + 64, :] = gone[h]

    ring_step(3)
    ring_step(4)
    ones8 = jnp.ones((8, 768), BF16)
    for cut, rows, p_rows in (
        (slice(0, PART), rings, proj),
        (slice(PART, HALF), rings_b, proj_b),
    ):
        w = rows[...].reshape(768, cut.stop - cut.start)
        part_fold = dot(p_rows[...], w) - mean_col * dot(ones8, w)[0:1]
        if cut.start == 0:
            q_scale = 0.125 * 1.4426950408889634
            part_fold = part_fold * jnp.where(iota((1, PART), 1) < 384, q_scale, 1.0)
        fold[:, cut] = part_fold.astype(BF16)
    serve(0)

    lane = iota((256, 128), 1)
    unit = onehot(lane == 0).astype(BF16)
    ones = jnp.ones((1024, 128), BF16)

    def give(p):
        return remote(mixed.at[p, 128:256], theirs.at[p], m_send.at[p], m_recv.at[p], sibling)

    def one_phase(p, carry):
        for slot in range(4):
            f_sib(slot, p).wait_recv()
        x = slots[:, :, p].reshape(1024, 256)
        y = dot(x, gram[...])
        var = jnp.sum(y * x.astype(F32), axis=1, keepdims=True)
        rstd = lax.rsqrt(jnp.maximum(var, 0.0) + 1e-05)
        kv = (dot(x, fold[:, 384:]) * rstd).astype(BF16)
        keys[...] = kv[:, 0:384]
        values[...] = kv[:, 384:768]
        queries[...] = (dot(x[0:256], fold[:, 0:384]) * rstd[0:256]).astype(BF16)
        mask = dead[p].reshape(1024, 128)
        for n in range(3):
            if n == 1:

                @pl.when(p < 3)
                def _():
                    serve(p + 1)

            cut = slice(128 * n, 128 * n + 128)
            k_pair = jnp.concatenate([keys[:, cut], mask], axis=1)
            v_pair = jnp.concatenate([values[:, cut], ones], axis=1)
            q_pair = queries[:, cut].astype(F32)
            both = []
            for e in range(2):
                q_head = jnp.where((lane >= 64) == (e == 1), q_pair, 0.0).astype(BF16)
                scores = dot_nt(jnp.concatenate([q_head, unit], axis=1), k_pair)
                highest = jnp.max(scores, axis=1, keepdims=True)
                weights = jnp.exp2(scores - highest).astype(BF16)
                result = dot(weights, v_pair)
                both.append(result[:, 0:128] / result[:, 128:256])
            mixed[p, :, cut] = jnp.where(lane < 64, both[0], both[1]).astype(BF16)
        give(p).start()
        return carry

    lax.fori_loop(0, 4, one_phase, 0)

    back = []
    j, lane = iota((32, 256), 0), iota((32, 256), 1)
    for h in range(2):
        blocks = []
        for i in range(8):
            p = ((j & 3) + phase[8 * h + i, 0]) & 3
            blocks.append(onehot(lane == p * 64 + i * 8 + (j >> 2)))
        live = flags[0, 0, 0:1, 256 * h : 256 * h + 256].astype(F32)
        back.append((jnp.concatenate(blocks, axis=0) * live).astype(BF16))
    for p in range(4):
        give(p).wait_recv()
    for h in range(2):
        a = mixed[:, 64 * h : 64 * h + 64].reshape(256, 384)
        b = theirs[:, 64 * h : 64 * h + 64].reshape(256, 384)
        a, b = dot(back[h], a), dot(back[h], b)
        lower = jnp.where(core == 0, a, b).astype(BF16).reshape(8, 32, 384)
        upper = jnp.where(core == 0, b, a).astype(BF16).reshape(8, 32, 384)
        out[8 * h : 8 * h + 8, :, 0:384] = lower
        out[8 * h : 8 * h + 8, :, 384:768] = upper

    for copy in z_copies + g_copies + [
        to_right, to_left, on_right, on_left, sib_left, sib_right, sib_on, sib_off,
        top_copy, left_copy, corner_copy,
    ]:
        copy.wait_send()
    for t in range(4):
        for n in range(4):
            ring(n, t).wait_send()
    for p in range(4):
        give(p).wait_send()
        f_two(p).wait_send()
        for slot in range(4):
            f_sib(slot, p).wait_send()

        @pl.when(place < 3)
        def _():
            f_right(p).wait_send()

        @pl.when(place > 0)
        def _():
            f_left(p).wait_send()

        @pl.when((place == 1) | (place == 2))
        def _():
            f_far(p).wait_send()


def local(feat_in, conv_weight, conv_bias, proj_weight, qkv_weight, tissue, phase):
    vmem = pl.BlockSpec(memory_space=pltpu.VMEM)
    dma = pltpu.SemaphoreType.DMA
    return pl.pallas_call(
        whole_kernel,
        out_shape=jax.ShapeDtypeStruct((16, 32, 768), BF16),
        in_specs=[vmem] * 5 + [pl.BlockSpec(memory_space=pltpu.SMEM), vmem],
        out_specs=vmem,
        scratch_shapes=[
            pltpu.VMEM((2, 17, 2, 5, 8, 256), F32),
            pltpu.VMEM((32, 256), BF16),
            pltpu.VMEM((40, 256), BF16),
            pltpu.VMEM((64, 256), BF16),
            pltpu.VMEM((4, 576, 256), BF16),
            pltpu.VMEM((2, 8, PART), BF16),
            pltpu.VMEM((16, 8, PART), BF16),
            pltpu.VMEM((NY, 96, PART), BF16),
            pltpu.VMEM((2, 8, REST), BF16),
            pltpu.VMEM((16, 8, REST), BF16),
            pltpu.VMEM((NY, 96, REST), BF16),
            pltpu.VMEM((256, 768), BF16),
            pltpu.VMEM((4, 2, 4, 128, 256), BF16),
            pltpu.VMEM((4, 2, 8, 512), BF16),
            pltpu.VMEM((2, 256, 256), BF16),
            pltpu.VMEM((256, HALF), BF16),
            pltpu.VMEM((256, 256), BF16),
            pltpu.VMEM((1024, 384), BF16),
            pltpu.VMEM((1024, 384), BF16),
            pltpu.VMEM((4, 4, 2, 128, 128), BF16),
            pltpu.VMEM((256, 384), BF16),
            pltpu.VMEM((4, 256, 384), BF16),
            pltpu.VMEM((4, 128, 384), BF16),
            dma((8,)), dma((8,)),
            dma((3,)), dma((3,)),
            dma((16,)), dma((16,)),
            dma((8,)), dma((8,)),
            dma((4, 4)), dma((4, 4)),
            dma((4, 4)), dma((4, 4)),
            dma((16,)), dma((16,)),
            dma((4, 4)), dma((4, 4)),
            dma((4,)), dma((4,)),
            dma((3,)),
        ],
        compiler_params=pltpu.CompilerParams(
            collective_id=0, has_side_effects=True, vmem_limit_bytes=VMEM_LIMIT
        ),
        name="whole",
    )(
        feat_in, conv_weight, conv_bias.reshape(1, 256), qkv_weight, proj_weight, phase, tissue
    )


def solution(mesh):
    in_specs = (
        P("row", "col", None),
        P("col", None),
        P(),
        P(),
        P("row", None),
        P("row", "col"),
        P("row", "col"),
    )
    out_specs = P("row", "col", None)
    return jax.shard_map(local, mesh=mesh, in_specs=in_specs, out_specs=out_specs, check_vma=False)
```

```python
import jax
import jax.numpy as jnp
from jax import lax
from jax.experimental import pallas as pl
from jax.experimental.pallas import tpu as pltpu
from jax.sharding import PartitionSpec as P

MESH = pl.DeviceIdType.MESH
F32 = jnp.float32
BF16 = jnp.bfloat16
ROWS = 128
COLS = 4
PLANE = 16
NY = 8
PAIR = 384
VMEM_LIMIT = 56 * 1024 * 1024


def iota(shape, dim):
    return lax.broadcasted_iota(jnp.int32, shape, dim)


def onehot(cond):
    return jnp.where(cond, 1.0, 0.0)


def dot(a, b):
    return jnp.dot(a, b, preferred_element_type=F32)


def dot_nt(a, b):
    return lax.dot_general(a, b, (((1,), (1,)), ((), ())), preferred_element_type=F32)


def dot_tn(a, b):
    return lax.dot_general(a, b, (((0,), (0,)), ((), ())), preferred_element_type=F32)


def remote(src, dst, send_sem, recv_sem, device):
    return pltpu.make_async_remote_copy(
        src_ref=src,
        dst_ref=dst,
        send_sem=send_sem,
        recv_sem=recv_sem,
        device_id=device,
        device_id_type=MESH,
    )


def greet(devices):
    barrier = pltpu.get_barrier_semaphore()
    for device in devices:
        pl.semaphore_signal(barrier, inc=1, device_id=device, device_id_type=MESH)
    pl.semaphore_wait(barrier, len(devices))


def whole_kernel(
    feat, cw, bias, w6, proj, phase, tissue, out,
    grid_in, ext, halo, top, cwg, wsend, wz, rings, slots, flags, orders,
    fold, gram, dead, mixed, theirs,
    cw_send, cw_recv, h_send, h_recv, z_send, z_recv, g_send, g_recv,
    f_send, f_recv, s_send, s_recv, y_send, y_recv, x_send, x_recv, m_send, m_recv, own_sem,
):
    row, col = lax.axis_index("row"), lax.axis_index("col")
    core = lax.rem(row, 2)
    base = row - lax.rem(row, PLANE)
    mine = row - base
    y_at = row // PLANE
    place = lax.rem(row // 2, 4)
    sibling = (row + 1 - 2 * core, col)
    right, left = lax.rem(col + 1, COLS), lax.rem(col + COLS - 1, COLS)
    across = lax.rem(col + 2, COLS)
    down, up = lax.rem(row + 1, ROWS), lax.rem(row + ROWS - 1, ROWS)

    def along_y(step):
        return (lax.rem(row + PLANE * step + ROWS, ROWS), col)

    plane = [(base + lax.rem(mine + k, PLANE), col) for k in range(1, PLANE)]
    greet(
        [(row, right), (row, left), (down, col), (up, col), (down, right), (up, left)]
        + [(row, across)]
        + [along_y(step) for step in (1, -1, 2, -2)]
        + plane
    )

    part = pl.multiple_of(core * 288, 32)

    def cw_piece(slot, start, size):
        return cwg.at[slot, pl.ds(pl.multiple_of(part + start, 16), size), :]

    def cw_copy(i, slot, start, size, device):
        piece = cw_piece(slot, start, size)
        return remote(piece, piece, cw_send.at[i], cw_recv.at[i], device)

    own_cw = pltpu.make_async_copy(cw, cwg.at[col], own_sem.at[0])
    own_cw.start()
    half = cw.at[pl.ds(part, 288), :]
    to_right = remote(half, cw_piece(col, 0, 288), cw_send.at[0], cw_recv.at[0], (row, right))
    to_left = remote(half, cw_piece(col, 0, 288), cw_send.at[1], cw_recv.at[1], (row, left))
    to_right.start()
    to_left.start()
    top_copy = remote(feat.at[31], top, h_send.at[0], h_recv.at[0], (down, col))
    top_copy.start()

    group = lax.rem(col, 3)
    for c in range(2):
        wsend[c] = jnp.zeros((8, PAIR), BF16)
        for j in range(3):
            at = pl.multiple_of(768 * j + 384 * c + 128 * group, 128)
            wsend[c, 0:6, 128 * j : 128 * j + 128] = w6[:, pl.ds(at, 128)]
    z_copies = []
    for k in range(1, PLANE):
        to_core = lax.rem(core + k, 2)
        copy = remote(
            wsend.at[to_core], wz.at[mine], z_send.at[k], z_recv.at[k], plane[k - 1]
        )
        copy.start()
        z_copies.append(copy)
    own_z = pltpu.make_async_copy(wsend.at[core], wz.at[mine], own_sem.at[1])
    own_z.start()

    o, c = iota((256, 256), 0), iota((256, 256), 1)
    k, si, sp = o & 7, (o >> 3) & 3, (o >> 5) & 1
    r = 2 * ((o >> 6) & 1) + (o >> 7)
    split = onehot(c == r * 64 + 8 * k + 2 * si + sp).astype(BF16)
    for g in range(8):
        x = feat[4 * g : 4 * g + 4].reshape(256, 256)
        y = dot(split, x).reshape(2, 2, 2, 4, 8, 256)
        grid_in[0, 2 * g : 2 * g + 2, 0, 0:4] = y[0, :, 0]
        grid_in[0, 2 * g : 2 * g + 2, 1, 1:5] = y[0, :, 1]
        grid_in[1, 2 * g + 1 : 2 * g + 3, 0, 0:4] = y[1, :, 0]
        grid_in[1, 2 * g + 1 : 2 * g + 3, 1, 1:5] = y[1, :, 1]

    for rp in range(2):
        for i in range(0, 16, 8):
            rows8 = [grid_in[rp, rp + i + e, 1, 4, 7:8, :] for e in range(8)]
            ext[16 * rp + i : 16 * rp + i + 8, :] = jnp.concatenate(rows8, axis=0).astype(BF16)
    left_copy = remote(ext, halo.at[0:32], h_send.at[1], h_recv.at[1], (row, right))
    left_copy.start()
    corner_copy = remote(
        ext.at[24:32], halo.at[32:40], h_send.at[2], h_recv.at[2], (down, right)
    )
    corner_copy.start()

    lane, sub = iota((8, 256), 1), iota((8, 256), 0)
    for h in range(2):
        blocks = []
        for p in range(4):
            for i in range(8):
                target = i * 32 + ((p - phase[8 * h + i, 0]) & 3) * 8
                blocks.append(onehot(lane == sub + target))
        order = jnp.concatenate(blocks, axis=0).astype(BF16)
        orders[h] = order
        j, c = iota((32, 256), 0), iota((32, 256), 1)
        pick = onehot(j == 4 * (c & 7) + ((c >> 3) & 3)).astype(BF16)
        live = dot(tissue[8 * h : 8 * h + 8, :].astype(F32).astype(BF16), pick)
        live = jnp.where(sub == (lane >> 5), live, 0.0).astype(BF16)
        live = dot(jnp.ones((8, 8), BF16), live).astype(BF16)
        flags[0, 0, :, 256 * h : 256 * h + 256] = dot_nt(live, order).astype(BF16)
    g_copies = []
    for dz in range(4):
        for dc in range(2):
            if dz or dc:
                n = 2 * dz + dc
                peer = row + 2 * (lax.rem(place + dz, 4) - place) + dc * (1 - 2 * core)
                copy = remote(
                    flags.at[0, 0], flags.at[(4 - dz) % 4, dc], g_send.at[n], g_recv.at[n], (peer, col)
                )
                copy.start()
                g_copies.append(copy)

    p32 = proj[...].astype(F32)
    mean_col = jnp.mean(p32, axis=1, keepdims=True)
    mean_row = dot_nt(jnp.ones((8, 768), BF16), proj[...])[0:1] * (1.0 / 768.0)
    gram[...] = (dot_nt(proj[...], proj[...]) * (1.0 / 768.0) - mean_col * mean_row).astype(BF16)

    to_right.wait_recv()
    on_right = cw_copy(2, left, 0, 144, (row, right))
    on_right.start()
    sib_left = cw_copy(4, left, 0, 288, sibling)
    sib_left.start()
    to_left.wait_recv()
    on_left = cw_copy(3, right, 144, 144, (row, left))
    on_left.start()
    sib_right = cw_copy(5, right, 0, 288, sibling)
    sib_right.start()

    own_z.wait()
    for copy in z_copies:
        copy.wait_recv()
    o, c = iota((96, 128), 0), iota((96, 128), 1)
    pack = onehot((o == 6 * (c >> 3) + (c & 7)) & ((c & 7) < 6)).astype(BF16)
    rings[y_at] = dot(pack, wz[...].reshape(128, PAIR)).astype(BF16)

    def y_copy(i, start, size, behind, step):
        piece = rings.at[lax.rem(y_at - behind + NY, NY), start : start + size]
        return remote(piece, piece, y_send.at[i], y_recv.at[i], along_y(step))

    y_near = [y_copy(i, 0, 96, 0, step) for i, step in enumerate((2, -2, 1, -1))]
    for copy in y_near:
        copy.start()

    top_copy.wait_recv()
    left_copy.wait_recv()
    corner_copy.wait_recv()
    inside = row > 0
    inner = col > 0
    o, c = iota((64, 64), 0), iota((64, 64), 1)
    split_row = onehot(c == 8 * (o & 7) + 2 * ((o >> 3) & 3) + (o >> 5)).astype(BF16)
    yt = jnp.where(inside, dot(split_row, top[...]), 0.0).reshape(2, 4, 8, 256)
    grid_in[1, 0, 0, 0:4] = yt[0]
    grid_in[1, 0, 1, 1:5] = yt[1]
    o, c = iota((264, 40), 0), iota((264, 40), 1)
    source = o >> 3
    source = jnp.where(source < 16, source, jnp.where(source == 16, 39, source - 1))
    spread = onehot((c == source) & ((o & 7) == 0)).astype(BF16)
    edge = jnp.where(inner, dot(spread, halo[...]), 0.0).reshape(33, 8, 256)
    first = iota((1, 8, 256), 1) == 0
    moved = pltpu.roll(grid_in[0, 0:16, 1, 4], 1, 1)
    grid_in[0, 0:16, 1, 0] = jnp.where(first, edge[0:16], moved)
    moved = pltpu.roll(grid_in[1, 0:17, 1, 4], 1, 1)
    keep = edge[16:33]
    keep = jnp.where((iota((17, 8, 256), 0) == 0) & jnp.logical_not(inside), 0.0, keep)
    grid_in[1, 0:17, 1, 0] = jnp.where(first, keep, moved)

    on_right.wait_recv()
    sib_on = cw_copy(6, across, 0, 144, sibling)
    sib_on.start()
    on_left.wait_recv()
    sib_off = cw_copy(7, across, 144, 144, sibling)
    sib_off.start()
    own_cw.wait()
    for copy in (sib_left, sib_right, sib_on, sib_off):
        copy.wait_recv()

    weights = cwg[...].reshape(2304, 256)
    for h in range(2):
        pieces = []
        for a in range(3):
            for b in range(3):
                rp, i0 = (0, 0) if a == 1 else (1, a // 2)
                sp, m0 = (0, 0) if b == 1 else (1, b // 2)
                window = grid_in[rp, i0 + 8 * h : i0 + 8 * h + 8, sp, m0 : m0 + 4]
                pieces.append(window.reshape(256, 256).astype(BF16))
        pre = dot(jnp.concatenate(pieces, axis=1), weights) + bias[...]
        features = jax.nn.gelu(pre).astype(BF16)
        f32 = features.astype(F32)
        spread_rows = jnp.sum(dot(features, gram[...]) * f32, axis=1, keepdims=True)
        f32 = f32 * lax.rsqrt(jnp.maximum(spread_rows, 0.0) + 1e-05)
        placed = dot(orders[h], f32.astype(BF16)).astype(BF16).reshape(4, 64, 256)
        slots[0, 0, :, 64 * h : 64 * h + 64, :] = placed

    def f_right(p):
        return remote(
            slots.at[0, 0, p], slots.at[3, 0, p], f_send.at[0, p], f_recv.at[3, p],
            (lax.rem(row + 2, ROWS), col),
        )

    def f_left(p):
        return remote(
            slots.at[0, 0, p], slots.at[1, 0, p], f_send.at[1, p], f_recv.at[1, p],
            (lax.rem(row + ROWS - 2, ROWS), col),
        )

    def f_two(p):
        return remote(
            slots.at[0, 0, p], slots.at[2, 0, p], f_send.at[2, p], f_recv.at[2, p],
            (row + 4 * jnp.where(place < 2, 1, -1), col),
        )

    def f_far(p):
        to = jnp.where(place == 2, 1, 3)
        return remote(
            slots.at[2, 0, p], slots.at[to, 0, p], f_send.at[3, p], f_recv.at[to, p],
            (row + 2 * jnp.where(place == 2, 1, -1), col),
        )

    def f_sib(slot, p):
        piece = slots.at[slot, 0, p]
        return remote(piece, slots.at[slot, 1, p], s_send.at[slot, p], s_recv.at[slot, p], sibling)

    def arrived(slot, p):
        piece = slots.at[slot, 0, p]
        return remote(piece, piece, f_send.at[0, p], f_recv.at[slot, p], sibling)

    for p in range(4):

        @pl.when(place < 3)
        def _():
            f_right(p).start()

        @pl.when(place > 0)
        def _():
            f_left(p).start()

        f_two(p).start()
        f_sib(0, p).start()

    def serve(p):
        arrived(2, p).wait_recv()

        @pl.when((place == 1) | (place == 2))
        def _():
            f_far(p).start()

        f_sib(2, p).start()
        for slot in (1, 3):
            arrived(slot, p).wait_recv()
            f_sib(slot, p).start()

    y_near[0].wait_recv()
    y_far = [y_copy(4, 0, 96, 2, 1), y_copy(6, 0, 48, 2, 2)]
    for copy in y_far:
        copy.start()
    y_near[1].wait_recv()
    y_back = [y_copy(5, 0, 96, -2, -1), y_copy(7, 48, 48, -2, -2)]
    for copy in y_back:
        copy.start()
    y_far = y_far + y_back

    for copy in g_copies:
        copy.wait_recv()
    lane128 = iota((512, 128), 1)
    first_row = onehot((iota((8, 128), 0) == 0) & (iota((8, 128), 1) == 0)).astype(BF16)
    for q in range(4):
        for c in range(2):
            live = dot_tn(flags[q, c], first_row)
            gone = jnp.where((lane128 == 0) , (live - 1.0) * 1e30, 0.0).astype(BF16)
            gone = gone.reshape(2, 4, 64, 128)
            for h in range(2):
                dead[:, q, c, 64 * h : 64 * h + 64, :] = gone[h]

    for copy in y_near[2:] + y_far:
        copy.wait_recv()
    w = rings[...].reshape(768, PAIR)
    folded = dot(proj[...], w) - mean_col * dot(jnp.ones((8, 768), BF16), w)[0:1]
    scale = jnp.where(iota((1, PAIR), 1) < 128, 0.125 * 1.4426950408889634, 1.0)
    fold[group] = (folded * scale).astype(BF16)

    x_copies = [
        (a, remote(fold.at[a % 3], fold.at[a % 3], x_send.at[b], x_recv.at[a % 3], (row, b)))
        for a, b in ((0, 1), (1, 0), (1, 2), (1, 3), (2, 1), (2, 3), (2, 0), (3, 2))
    ]
    for a, copy in x_copies:
        pl.when(col == a)(copy.start)
    serve(0)
    for g in range(3):
        pl.when(group != g)(remote(
            fold.at[g], fold.at[g], x_send.at[0], x_recv.at[g], sibling
        ).wait_recv)

    lane = iota((256, 128), 1)
    unit = onehot(lane == 0).astype(BF16)
    ones = jnp.ones((1024, 128), BF16)

    def give(p):
        return remote(mixed.at[p, 128:256], theirs.at[p], m_send.at[p], m_recv.at[p], sibling)

    def one_phase(p, carry):
        for slot in range(4):
            f_sib(slot, p).wait_recv()
        x = slots[:, :, p].reshape(1024, 256)
        mask = dead[p].reshape(1024, 128)
        for n in range(3):
            if n == 1:

                @pl.when(p < 3)
                def _():
                    serve(p + 1)

            cut = slice(128 * n, 128 * n + 128)
            kv = dot(x, fold[n, :, 128:384]).astype(BF16)
            k_pair = jnp.concatenate([kv[:, 0:128], mask], axis=1)
            v_pair = jnp.concatenate([kv[:, 128:256], ones], axis=1)
            q_pair = dot(x[0:256], fold[n, :, 0:128])
            both = []
            for e in range(2):
                q_head = jnp.where((lane >= 64) == (e == 1), q_pair, 0.0).astype(BF16)
                scores = dot_nt(jnp.concatenate([q_head, unit], axis=1), k_pair)
                highest = jnp.max(scores, axis=1, keepdims=True)
                weights = jnp.exp2(scores - highest).astype(BF16)
                result = dot(weights, v_pair)
                both.append(result[:, 0:128] / result[:, 128:256])
            mixed[p, :, cut] = jnp.where(lane < 64, both[0], both[1]).astype(BF16)
        give(p).start()
        return carry

    lax.fori_loop(0, 4, one_phase, 0)

    back = []
    j, lane = iota((32, 256), 0), iota((32, 256), 1)
    for h in range(2):
        blocks = []
        for i in range(8):
            p = ((j & 3) + phase[8 * h + i, 0]) & 3
            blocks.append(onehot(lane == p * 64 + i * 8 + (j >> 2)))
        live = flags[0, 0, 0:1, 256 * h : 256 * h + 256].astype(F32)
        back.append((jnp.concatenate(blocks, axis=0) * live).astype(BF16))
    for p in range(4):
        give(p).wait_recv()
    for h in range(2):
        a = mixed[:, 64 * h : 64 * h + 64].reshape(256, 384)
        b = theirs[:, 64 * h : 64 * h + 64].reshape(256, 384)
        a, b = dot(back[h], a), dot(back[h], b)
        lower = jnp.where(core == 0, a, b).astype(BF16).reshape(8, 32, 384)
        upper = jnp.where(core == 0, b, a).astype(BF16).reshape(8, 32, 384)
        out[8 * h : 8 * h + 8, :, 0:384] = lower
        out[8 * h : 8 * h + 8, :, 384:768] = upper

    for copy in z_copies + g_copies + [
        to_right, to_left, on_right, on_left, sib_left, sib_right, sib_on, sib_off,
        top_copy, left_copy, corner_copy,
    ]:
        copy.wait_send()
    for copy in y_near + y_far:
        copy.wait_send()
    for a, copy in x_copies:
        pl.when(col == a)(copy.wait_send)
    for p in range(4):
        give(p).wait_send()
        f_two(p).wait_send()
        for slot in range(4):
            f_sib(slot, p).wait_send()

        @pl.when(place < 3)
        def _():
            f_right(p).wait_send()

        @pl.when(place > 0)
        def _():
            f_left(p).wait_send()

        @pl.when((place == 1) | (place == 2))
        def _():
            f_far(p).wait_send()


def local(feat_in, conv_weight, conv_bias, proj_weight, qkv_weight, tissue, phase):
    vmem = pl.BlockSpec(memory_space=pltpu.VMEM)
    dma = pltpu.SemaphoreType.DMA
    return pl.pallas_call(
        whole_kernel,
        out_shape=jax.ShapeDtypeStruct((16, 32, 768), BF16),
        in_specs=[vmem] * 5 + [pl.BlockSpec(memory_space=pltpu.SMEM), vmem],
        out_specs=vmem,
        scratch_shapes=[
            pltpu.VMEM((2, 17, 2, 5, 8, 256), F32),
            pltpu.VMEM((32, 256), BF16),
            pltpu.VMEM((40, 256), BF16),
            pltpu.VMEM((64, 256), BF16),
            pltpu.VMEM((4, 576, 256), BF16),
            pltpu.VMEM((2, 8, PAIR), BF16),
            pltpu.VMEM((16, 8, PAIR), BF16),
            pltpu.VMEM((NY, 96, PAIR), BF16),
            pltpu.VMEM((4, 2, 4, 128, 256), BF16),
            pltpu.VMEM((4, 2, 8, 512), BF16),
            pltpu.VMEM((2, 256, 256), BF16),
            pltpu.VMEM((3, 256, PAIR), BF16),
            pltpu.VMEM((256, 256), BF16),
            pltpu.VMEM((4, 4, 2, 128, 128), BF16),
            pltpu.VMEM((4, 256, 384), BF16),
            pltpu.VMEM((4, 128, 384), BF16),
            dma((8,)), dma((8,)),
            dma((3,)), dma((3,)),
            dma((16,)), dma((16,)),
            dma((8,)), dma((8,)),
            dma((4, 4)), dma((4, 4)),
            dma((4, 4)), dma((4, 4)),
            dma((8,)), dma((8,)),
            dma((4,)), dma((3,)),
            dma((4,)), dma((4,)),
            dma((2,)),
        ],
        compiler_params=pltpu.CompilerParams(
            collective_id=0, has_side_effects=True, vmem_limit_bytes=VMEM_LIMIT
        ),
        name="whole",
    )(
        feat_in, conv_weight, conv_bias.reshape(1, 256), qkv_weight, proj_weight, phase, tissue
    )


def solution(mesh):
    in_specs = (
        P("row", "col", None),
        P("col", None),
        P(),
        P(),
        P("row", None),
        P("row", "col"),
        P("row", "col"),
    )
    out_specs = P("row", "col", None)
    return jax.shard_map(local, mesh=mesh, in_specs=in_specs, out_specs=out_specs, check_vma=False)
```

```python
import jax
import jax.numpy as jnp
from jax import lax
from jax.experimental import pallas as pl
from jax.experimental.pallas import tpu as pltpu
from jax.sharding import PartitionSpec as P

MESH = pl.DeviceIdType.MESH
F32 = jnp.float32
BF16 = jnp.bfloat16
ROWS = 128
COLS = 4
PLANE = 16
NY = 8
PAIR = 384
VMEM_LIMIT = 56 * 1024 * 1024


def iota(shape, dim):
    return lax.broadcasted_iota(jnp.int32, shape, dim)


def onehot(cond):
    return jnp.where(cond, 1.0, 0.0)


def dot(a, b):
    return jnp.dot(a, b, preferred_element_type=F32)


def dot_nt(a, b):
    return lax.dot_general(a, b, (((1,), (1,)), ((), ())), preferred_element_type=F32)


def dot_tn(a, b):
    return lax.dot_general(a, b, (((0,), (0,)), ((), ())), preferred_element_type=F32)


def remote(src, dst, send_sem, recv_sem, device):
    return pltpu.make_async_remote_copy(
        src_ref=src,
        dst_ref=dst,
        send_sem=send_sem,
        recv_sem=recv_sem,
        device_id=device,
        device_id_type=MESH,
    )


def greet(devices):
    barrier = pltpu.get_barrier_semaphore()
    for device in devices:
        pl.semaphore_signal(barrier, inc=1, device_id=device, device_id_type=MESH)
    pl.semaphore_wait(barrier, len(devices))


def whole_kernel(
    feat, cw, bias, w6, proj, phase, tissue, out,
    grid_in, ext, halo, top, cwg, wsend, wz, rings, slots, flags, orders,
    fold, gram, dead, mixed, theirs,
    cw_send, cw_recv, h_send, h_recv, z_send, z_recv, g_send, g_recv,
    f_send, f_recv, s_send, s_recv, y_send, y_recv, x_send, x_recv, m_send, m_recv, own_sem,
):
    row, col = lax.axis_index("row"), lax.axis_index("col")
    core = lax.rem(row, 2)
    base = row - lax.rem(row, PLANE)
    mine = row - base
    y_at = row // PLANE
    place = lax.rem(row // 2, 4)
    sibling = (row + 1 - 2 * core, col)
    right, left = lax.rem(col + 1, COLS), lax.rem(col + COLS - 1, COLS)
    across = lax.rem(col + 2, COLS)
    down, up = lax.rem(row + 1, ROWS), lax.rem(row + ROWS - 1, ROWS)

    def along_y(step):
        return (lax.rem(row + PLANE * step + ROWS, ROWS), col)

    plane = [(base + lax.rem(mine + k, PLANE), col) for k in range(1, PLANE)]
    greet(
        [(row, right), (row, left), (down, col), (up, col), (down, right), (up, left)]
        + [(row, across)]
        + [along_y(step) for step in (1, -1, 2, -2)]
        + plane
    )

    part = pl.multiple_of(core * 288, 32)

    def cw_piece(slot, start, size):
        return cwg.at[slot, pl.ds(pl.multiple_of(part + start, 16), size), :]

    def cw_copy(i, slot, start, size, device):
        piece = cw_piece(slot, start, size)
        return remote(piece, piece, cw_send.at[i], cw_recv.at[i], device)

    own_cw = pltpu.make_async_copy(cw, cwg.at[col], own_sem.at[0])
    own_cw.start()
    half = cw.at[pl.ds(part, 288), :]
    to_right = remote(half, cw_piece(col, 0, 288), cw_send.at[0], cw_recv.at[0], (row, right))
    to_left = remote(half, cw_piece(col, 0, 288), cw_send.at[1], cw_recv.at[1], (row, left))
    to_right.start()
    to_left.start()
    top_copy = remote(feat.at[31], top, h_send.at[0], h_recv.at[0], (down, col))
    top_copy.start()

    group = lax.rem(col, 3)
    for c in range(2):
        wsend[c] = jnp.zeros((8, PAIR), BF16)
        for j in range(3):
            at = pl.multiple_of(768 * j + 384 * c + 128 * group, 128)
            wsend[c, 0:6, 128 * j : 128 * j + 128] = w6[:, pl.ds(at, 128)]
    z_copies = []
    for k in range(1, PLANE):
        to_core = lax.rem(core + k, 2)
        copy = remote(
            wsend.at[to_core], wz.at[mine], z_send.at[k], z_recv.at[k], plane[k - 1]
        )
        copy.start()
        z_copies.append(copy)
    own_z = pltpu.make_async_copy(wsend.at[core], wz.at[mine], own_sem.at[1])
    own_z.start()

    o, c = iota((256, 256), 0), iota((256, 256), 1)
    k, si, sp = o & 7, (o >> 3) & 3, (o >> 5) & 1
    r = 2 * ((o >> 6) & 1) + (o >> 7)
    split = onehot(c == r * 64 + 8 * k + 2 * si + sp).astype(BF16)
    for g in range(8):
        x = feat[4 * g : 4 * g + 4].reshape(256, 256)
        y = dot(split, x).reshape(2, 2, 2, 4, 8, 256)
        grid_in[0, 2 * g : 2 * g + 2, 0, 0:4] = y[0, :, 0]
        grid_in[0, 2 * g : 2 * g + 2, 1, 1:5] = y[0, :, 1]
        grid_in[1, 2 * g + 1 : 2 * g + 3, 0, 0:4] = y[1, :, 0]
        grid_in[1, 2 * g + 1 : 2 * g + 3, 1, 1:5] = y[1, :, 1]

    for rp in range(2):
        for i in range(0, 16, 8):
            rows8 = [grid_in[rp, rp + i + e, 1, 4, 7:8, :] for e in range(8)]
            ext[16 * rp + i : 16 * rp + i + 8, :] = jnp.concatenate(rows8, axis=0).astype(BF16)
    left_copy = remote(ext, halo.at[0:32], h_send.at[1], h_recv.at[1], (row, right))
    left_copy.start()
    corner_copy = remote(
        ext.at[24:32], halo.at[32:40], h_send.at[2], h_recv.at[2], (down, right)
    )
    corner_copy.start()

    own_z.wait()
    for copy in z_copies:
        copy.wait_recv()
    o, c = iota((96, 128), 0), iota((96, 128), 1)
    pack = onehot((o == 6 * (c >> 3) + (c & 7)) & ((c & 7) < 6)).astype(BF16)
    rings[y_at] = dot(pack, wz[...].reshape(128, PAIR)).astype(BF16)

    def y_copy(i, start, size, behind, step):
        piece = rings.at[lax.rem(y_at - behind + NY, NY), start : start + size]
        return remote(piece, piece, y_send.at[i], y_recv.at[i], along_y(step))

    y_near = [y_copy(i, 0, 96, 0, step) for i, step in enumerate((2, -2, 1, -1))]
    for copy in y_near:
        copy.start()

    to_right.wait_recv()
    on_right = cw_copy(2, left, 0, 144, (row, right))
    on_right.start()
    sib_left = cw_copy(4, left, 0, 288, sibling)
    sib_left.start()
    to_left.wait_recv()
    on_left = cw_copy(3, right, 144, 144, (row, left))
    on_left.start()
    sib_right = cw_copy(5, right, 0, 288, sibling)
    sib_right.start()

    lane, sub = iota((8, 256), 1), iota((8, 256), 0)
    for h in range(2):
        blocks = []
        for p in range(4):
            for i in range(8):
                target = i * 32 + ((p - phase[8 * h + i, 0]) & 3) * 8
                blocks.append(onehot(lane == sub + target))
        order = jnp.concatenate(blocks, axis=0).astype(BF16)
        orders[h] = order
        j, c = iota((32, 256), 0), iota((32, 256), 1)
        pick = onehot(j == 4 * (c & 7) + ((c >> 3) & 3)).astype(BF16)
        live = dot(tissue[8 * h : 8 * h + 8, :].astype(F32).astype(BF16), pick)
        live = jnp.where(sub == (lane >> 5), live, 0.0).astype(BF16)
        live = dot(jnp.ones((8, 8), BF16), live).astype(BF16)
        flags[0, 0, :, 256 * h : 256 * h + 256] = dot_nt(live, order).astype(BF16)
    g_copies = []
    for dz in range(4):
        for dc in range(2):
            if dz or dc:
                n = 2 * dz + dc
                peer = row + 2 * (lax.rem(place + dz, 4) - place) + dc * (1 - 2 * core)
                copy = remote(
                    flags.at[0, 0], flags.at[(4 - dz) % 4, dc], g_send.at[n], g_recv.at[n], (peer, col)
                )
                copy.start()
                g_copies.append(copy)

    p32 = proj[...].astype(F32)
    mean_col = jnp.mean(p32, axis=1, keepdims=True)
    mean_row = dot_nt(jnp.ones((8, 768), BF16), proj[...])[0:1] * (1.0 / 768.0)
    gram[...] = (dot_nt(proj[...], proj[...]) * (1.0 / 768.0) - mean_col * mean_row).astype(BF16)

    top_copy.wait_recv()
    left_copy.wait_recv()
    corner_copy.wait_recv()
    inside = row > 0
    inner = col > 0
    o, c = iota((64, 64), 0), iota((64, 64), 1)
    split_row = onehot(c == 8 * (o & 7) + 2 * ((o >> 3) & 3) + (o >> 5)).astype(BF16)
    yt = jnp.where(inside, dot(split_row, top[...]), 0.0).reshape(2, 4, 8, 256)
    grid_in[1, 0, 0, 0:4] = yt[0]
    grid_in[1, 0, 1, 1:5] = yt[1]
    o, c = iota((264, 40), 0), iota((264, 40), 1)
    source = o >> 3
    source = jnp.where(source < 16, source, jnp.where(source == 16, 39, source - 1))
    spread = onehot((c == source) & ((o & 7) == 0)).astype(BF16)
    edge = jnp.where(inner, dot(spread, halo[...]), 0.0).reshape(33, 8, 256)
    first = iota((1, 8, 256), 1) == 0
    moved = pltpu.roll(grid_in[0, 0:16, 1, 4], 1, 1)
    grid_in[0, 0:16, 1, 0] = jnp.where(first, edge[0:16], moved)
    moved = pltpu.roll(grid_in[1, 0:17, 1, 4], 1, 1)
    keep = edge[16:33]
    keep = jnp.where((iota((17, 8, 256), 0) == 0) & jnp.logical_not(inside), 0.0, keep)
    grid_in[1, 0:17, 1, 0] = jnp.where(first, keep, moved)

    on_right.wait_recv()
    sib_on = cw_copy(6, across, 0, 144, sibling)
    sib_on.start()
    on_left.wait_recv()
    sib_off = cw_copy(7, across, 144, 144, sibling)
    sib_off.start()
    own_cw.wait()
    for copy in (sib_left, sib_right, sib_on, sib_off):
        copy.wait_recv()

    y_near[0].wait_recv()
    y_far = [y_copy(4, 0, 96, 2, 1), y_copy(6, 0, 48, 2, 2)]
    for copy in y_far:
        copy.start()
    y_near[1].wait_recv()
    y_back = [y_copy(5, 0, 96, -2, -1), y_copy(7, 48, 48, -2, -2)]
    for copy in y_back:
        copy.start()
    y_far = y_far + y_back

    weights = cwg[...].reshape(2304, 256)
    for h in range(2):
        pieces = []
        for a in range(3):
            for b in range(3):
                rp, i0 = (0, 0) if a == 1 else (1, a // 2)
                sp, m0 = (0, 0) if b == 1 else (1, b // 2)
                window = grid_in[rp, i0 + 8 * h : i0 + 8 * h + 8, sp, m0 : m0 + 4]
                pieces.append(window.reshape(256, 256).astype(BF16))
        pre = dot(jnp.concatenate(pieces, axis=1), weights) + bias[...]
        features = jax.nn.gelu(pre).astype(BF16)
        f32 = features.astype(F32)
        spread_rows = jnp.sum(dot(features, gram[...]) * f32, axis=1, keepdims=True)
        f32 = f32 * lax.rsqrt(jnp.maximum(spread_rows, 0.0) + 1e-05)
        placed = dot(orders[h], f32.astype(BF16)).astype(BF16).reshape(4, 64, 256)
        slots[0, 0, :, 64 * h : 64 * h + 64, :] = placed

    def f_right(p):
        return remote(
            slots.at[0, 0, p], slots.at[3, 0, p], f_send.at[0, p], f_recv.at[3, p],
            (lax.rem(row + 2, ROWS), col),
        )

    def f_left(p):
        return remote(
            slots.at[0, 0, p], slots.at[1, 0, p], f_send.at[1, p], f_recv.at[1, p],
            (lax.rem(row + ROWS - 2, ROWS), col),
        )

    def f_two(p):
        return remote(
            slots.at[0, 0, p], slots.at[2, 0, p], f_send.at[2, p], f_recv.at[2, p],
            (row + 4 * jnp.where(place < 2, 1, -1), col),
        )

    def f_far(p):
        to = jnp.where(place == 2, 1, 3)
        return remote(
            slots.at[2, 0, p], slots.at[to, 0, p], f_send.at[3, p], f_recv.at[to, p],
            (row + 2 * jnp.where(place == 2, 1, -1), col),
        )

    def f_sib(slot, p):
        piece = slots.at[slot, 0, p]
        return remote(piece, slots.at[slot, 1, p], s_send.at[slot, p], s_recv.at[slot, p], sibling)

    def arrived(slot, p):
        piece = slots.at[slot, 0, p]
        return remote(piece, piece, f_send.at[0, p], f_recv.at[slot, p], sibling)

    for p in range(4):

        @pl.when(place < 3)
        def _():
            f_right(p).start()

        @pl.when(place > 0)
        def _():
            f_left(p).start()

        f_two(p).start()
        f_sib(0, p).start()

    def serve(p):
        arrived(2, p).wait_recv()

        @pl.when((place == 1) | (place == 2))
        def _():
            f_far(p).start()

        f_sib(2, p).start()
        for slot in (1, 3):
            arrived(slot, p).wait_recv()
            f_sib(slot, p).start()

    for copy in y_near[2:] + y_far:
        copy.wait_recv()
    w = rings[...].reshape(768, PAIR)
    folded = dot(proj[...], w) - mean_col * dot(jnp.ones((8, 768), BF16), w)[0:1]
    scale = jnp.where(iota((1, PAIR), 1) < 128, 0.125 * 1.4426950408889634, 1.0)
    fold[group] = (folded * scale).astype(BF16)

    x_copies = [
        (a, remote(fold.at[a % 3], fold.at[a % 3], x_send.at[b], x_recv.at[a % 3], (row, b)))
        for a, b in ((0, 1), (1, 0), (1, 2), (1, 3), (2, 1), (2, 3), (2, 0), (3, 2))
    ]
    for a, copy in x_copies:
        pl.when(col == a)(copy.start)
    for copy in g_copies:
        copy.wait_recv()
    lane128 = iota((512, 128), 1)
    first_row = onehot((iota((8, 128), 0) == 0) & (iota((8, 128), 1) == 0)).astype(BF16)
    for q in range(4):
        for c in range(2):
            live = dot_tn(flags[q, c], first_row)
            gone = jnp.where((lane128 == 0) , (live - 1.0) * 1e30, 0.0).astype(BF16)
            gone = gone.reshape(2, 4, 64, 128)
            for h in range(2):
                dead[:, q, c, 64 * h : 64 * h + 64, :] = gone[h]

    serve(0)
    lane = iota((256, 128), 1)
    unit = onehot(iota((512, 128), 1) == 0).astype(BF16)
    ones = jnp.ones((16, 1024), BF16)

    def give(p):
        return remote(mixed.at[p, :, 128:256], theirs.at[p], m_send.at[p], m_recv.at[p], sibling)

    def item(p, n):
        x = slots[:, :, p].reshape(1024, 256)
        mask = dead[p].reshape(1024, 128)
        kv = dot(x, fold[n, :, 128:384])
        keys = jnp.concatenate([kv[:, 0:128].astype(BF16), mask], axis=1)
        values = jnp.concatenate([kv[:, 128:256].T.astype(BF16), ones], axis=0)
        q_pair = dot(x[0:256], fold[n, :, 0:128])
        heads = jnp.concatenate(
            [jnp.where(lane < 64, q_pair, 0.0), jnp.where(lane < 64, 0.0, q_pair)], axis=0
        ).astype(BF16)
        scores = dot_nt(keys, jnp.concatenate([heads, unit], axis=1))
        highest = jnp.max(scores, axis=0, keepdims=True)
        weights = jnp.exp2(scores - highest).astype(BF16)
        result = dot(values, weights)
        result = result[0:128] / result[128:129]
        upper = iota((128, 256), 0) < 64
        mixed[p, n] = jnp.where(upper, result[:, 0:256], result[:, 256:512]).T.astype(BF16)

    def first(p):
        for slot in range(4):
            f_sib(slot, p).wait_recv()
        item(p, group)

    def early(p, carry):
        first(p)

        @pl.when(p == 0)
        def _():
            serve(1)

        return carry

    lax.fori_loop(0, 2, early, 0)

    for g in range(3):
        pl.when(group != g)(remote(
            fold.at[g], fold.at[g], x_send.at[0], x_recv.at[g], sibling
        ).wait_recv)

    def late(p, carry):
        @pl.when(p >= 2)
        def _():
            first(p)

        @pl.when(p == 2)
        def _():
            serve(3)

        item(p, lax.rem(group + 1, 3))

        @pl.when(p == 0)
        def _():
            serve(2)

        item(p, lax.rem(group + 2, 3))
        give(p).start()
        return carry

    lax.fori_loop(0, 4, late, 0)

    back = []
    j, lane = iota((32, 256), 0), iota((32, 256), 1)
    for h in range(2):
        blocks = []
        for i in range(8):
            p = ((j & 3) + phase[8 * h + i, 0]) & 3
            blocks.append(onehot(lane == p * 64 + i * 8 + (j >> 2)))
        live = flags[0, 0, 0:1, 256 * h : 256 * h + 256].astype(F32)
        back.append((jnp.concatenate(blocks, axis=0) * live).astype(BF16))
    for p in range(4):
        give(p).wait_recv()
    for h in range(2):
        a, b = (
            jnp.concatenate(
                [dot(back[h], m[:, n, 64 * h : 64 * h + 64].reshape(256, 128)) for n in range(3)],
                axis=1,
            )
            for m in (mixed, theirs)
        )
        lower = jnp.where(core == 0, a, b).astype(BF16).reshape(8, 32, 384)
        upper = jnp.where(core == 0, b, a).astype(BF16).reshape(8, 32, 384)
        out[8 * h : 8 * h + 8, :, 0:384] = lower
        out[8 * h : 8 * h + 8, :, 384:768] = upper

    for copy in z_copies + g_copies + [
        to_right, to_left, on_right, on_left, sib_left, sib_right, sib_on, sib_off,
        top_copy, left_copy, corner_copy,
    ]:
        copy.wait_send()
    for copy in y_near + y_far:
        copy.wait_send()
    for a, copy in x_copies:
        pl.when(col == a)(copy.wait_send)
    for p in range(4):
        give(p).wait_send()
        f_two(p).wait_send()
        for slot in range(4):
            f_sib(slot, p).wait_send()

        @pl.when(place < 3)
        def _():
            f_right(p).wait_send()

        @pl.when(place > 0)
        def _():
            f_left(p).wait_send()

        @pl.when((place == 1) | (place == 2))
        def _():
            f_far(p).wait_send()


def local(feat_in, conv_weight, conv_bias, proj_weight, qkv_weight, tissue, phase):
    vmem = pl.BlockSpec(memory_space=pltpu.VMEM)
    dma = pltpu.SemaphoreType.DMA
    return pl.pallas_call(
        whole_kernel,
        out_shape=jax.ShapeDtypeStruct((16, 32, 768), BF16),
        in_specs=[vmem] * 5 + [pl.BlockSpec(memory_space=pltpu.SMEM), vmem],
        out_specs=vmem,
        scratch_shapes=[
            pltpu.VMEM((2, 17, 2, 5, 8, 256), F32),
            pltpu.VMEM((32, 256), BF16),
            pltpu.VMEM((40, 256), BF16),
            pltpu.VMEM((64, 256), BF16),
            pltpu.VMEM((4, 576, 256), BF16),
            pltpu.VMEM((2, 8, PAIR), BF16),
            pltpu.VMEM((16, 8, PAIR), BF16),
            pltpu.VMEM((NY, 96, PAIR), BF16),
            pltpu.VMEM((4, 2, 4, 128, 256), BF16),
            pltpu.VMEM((4, 2, 8, 512), BF16),
            pltpu.VMEM((2, 256, 256), BF16),
            pltpu.VMEM((3, 256, PAIR), BF16),
            pltpu.VMEM((256, 256), BF16),
            pltpu.VMEM((4, 4, 2, 128, 128), BF16),
            pltpu.VMEM((4, 3, 256, 128), BF16),
            pltpu.VMEM((4, 3, 128, 128), BF16),
            dma((8,)), dma((8,)),
            dma((3,)), dma((3,)),
            dma((16,)), dma((16,)),
            dma((8,)), dma((8,)),
            dma((4, 4)), dma((4, 4)),
            dma((4, 4)), dma((4, 4)),
            dma((8,)), dma((8,)),
            dma((4,)), dma((3,)),
            dma((4,)), dma((4,)),
            dma((2,)),
        ],
        compiler_params=pltpu.CompilerParams(
            collective_id=0, has_side_effects=True, vmem_limit_bytes=VMEM_LIMIT
        ),
        name="whole",
    )(
        feat_in, conv_weight, conv_bias.reshape(1, 256), qkv_weight, proj_weight, phase, tissue
    )


def solution(mesh):
    in_specs = (
        P("row", "col", None),
        P("col", None),
        P(),
        P(),
        P("row", None),
        P("row", "col"),
        P("row", "col"),
    )
    out_specs = P("row", "col", None)
    return jax.shard_map(local, mesh=mesh, in_specs=in_specs, out_specs=out_specs, check_vma=False)
```

```python
import jax
import jax.numpy as jnp
from jax import lax
from jax.experimental import pallas as pl
from jax.experimental.pallas import tpu as pltpu
from jax.sharding import PartitionSpec as P

MESH = pl.DeviceIdType.MESH
F32 = jnp.float32
BF16 = jnp.bfloat16
ROWS = 128
COLS = 4
PLANE = 16
NY = 8
PAIR = 384
VMEM_LIMIT = 56 * 1024 * 1024


def iota(shape, dim):
    return lax.broadcasted_iota(jnp.int32, shape, dim)


def onehot(cond):
    return jnp.where(cond, 1.0, 0.0)


def dot(a, b):
    return jnp.dot(a, b, preferred_element_type=F32)


def dot_nt(a, b):
    return lax.dot_general(a, b, (((1,), (1,)), ((), ())), preferred_element_type=F32)


def dot_tn(a, b):
    return lax.dot_general(a, b, (((0,), (0,)), ((), ())), preferred_element_type=F32)


def remote(src, dst, send_sem, recv_sem, device):
    return pltpu.make_async_remote_copy(
        src_ref=src,
        dst_ref=dst,
        send_sem=send_sem,
        recv_sem=recv_sem,
        device_id=device,
        device_id_type=MESH,
    )


def greet(devices):
    barrier = pltpu.get_barrier_semaphore()
    for device in devices:
        pl.semaphore_signal(barrier, inc=1, device_id=device, device_id_type=MESH)
    pl.semaphore_wait(barrier, len(devices))


def whole_kernel(
    feat, cw, bias, w6, proj, phase, tissue, out,
    grid_in, ext, halo, top, cwg, wsend, wz, rings, slots, flags, orders,
    fold, gram, dead, mixed, theirs,
    cw_send, cw_recv, h_send, h_recv, z_send, z_recv, g_send, g_recv,
    f_send, f_recv, s_send, s_recv, y_send, y_recv, x_send, x_recv, m_send, m_recv, own_sem,
):
    row, col = lax.axis_index("row"), lax.axis_index("col")
    core = lax.rem(row, 2)
    base = row - lax.rem(row, PLANE)
    mine = row - base
    y_at = row // PLANE
    place = lax.rem(row // 2, 4)
    sibling = (row + 1 - 2 * core, col)
    right, left = lax.rem(col + 1, COLS), lax.rem(col + COLS - 1, COLS)
    across = lax.rem(col + 2, COLS)
    down, up = lax.rem(row + 1, ROWS), lax.rem(row + ROWS - 1, ROWS)

    def along_y(step):
        return (lax.rem(row + PLANE * step + ROWS, ROWS), col)

    plane = [(base + lax.rem(mine + k, PLANE), col) for k in range(1, PLANE)]
    greet(
        [(row, right), (row, left), (down, col), (up, col), (down, right), (up, left)]
        + [(row, across)]
        + [along_y(step) for step in (1, -1, 2, -2)]
        + plane
    )

    part = pl.multiple_of(core * 288, 32)

    def cw_piece(slot, start, size):
        return cwg.at[slot, pl.ds(pl.multiple_of(part + start, 16), size), :]

    def cw_copy(i, slot, start, size, device):
        piece = cw_piece(slot, start, size)
        return remote(piece, piece, cw_send.at[i], cw_recv.at[i], device)

    own_cw = pltpu.make_async_copy(cw, cwg.at[col], own_sem.at[0])
    own_cw.start()
    half = cw.at[pl.ds(part, 288), :]
    to_right = remote(half, cw_piece(col, 0, 288), cw_send.at[0], cw_recv.at[0], (row, right))
    to_left = remote(half, cw_piece(col, 0, 288), cw_send.at[1], cw_recv.at[1], (row, left))
    to_right.start()
    to_left.start()
    top_copy = remote(feat.at[31], top, h_send.at[0], h_recv.at[0], (down, col))
    top_copy.start()

    group = lax.rem(col, 3)
    for c in range(2):
        wsend[c] = jnp.zeros((8, PAIR), BF16)
        for j in range(3):
            at = pl.multiple_of(768 * j + 384 * c + 128 * group, 128)
            wsend[c, 0:6, 128 * j : 128 * j + 128] = w6[:, pl.ds(at, 128)]
    z_copies = []
    for k in range(1, PLANE):
        to_core = lax.rem(core + k, 2)
        copy = remote(
            wsend.at[to_core], wz.at[mine], z_send.at[k], z_recv.at[k], plane[k - 1]
        )
        copy.start()
        z_copies.append(copy)
    own_z = pltpu.make_async_copy(wsend.at[core], wz.at[mine], own_sem.at[1])
    own_z.start()

    o, c = iota((256, 256), 0), iota((256, 256), 1)
    k, si, sp = o & 7, (o >> 3) & 3, (o >> 5) & 1
    r = 2 * ((o >> 6) & 1) + (o >> 7)
    split = onehot(c == r * 64 + 8 * k + 2 * si + sp).astype(BF16)
    for g in range(8):
        x = feat[4 * g : 4 * g + 4].reshape(256, 256)
        y = dot(split, x).reshape(2, 2, 2, 4, 8, 256)
        grid_in[0, 2 * g : 2 * g + 2, 0, 0:4] = y[0, :, 0]
        grid_in[0, 2 * g : 2 * g + 2, 1, 1:5] = y[0, :, 1]
        grid_in[1, 2 * g + 1 : 2 * g + 3, 0, 0:4] = y[1, :, 0]
        grid_in[1, 2 * g + 1 : 2 * g + 3, 1, 1:5] = y[1, :, 1]

    for rp in range(2):
        for i in range(0, 16, 8):
            rows8 = [grid_in[rp, rp + i + e, 1, 4, 7:8, :] for e in range(8)]
            ext[16 * rp + i : 16 * rp + i + 8, :] = jnp.concatenate(rows8, axis=0).astype(BF16)
    left_copy = remote(ext, halo.at[0:32], h_send.at[1], h_recv.at[1], (row, right))
    left_copy.start()
    corner_copy = remote(
        ext.at[24:32], halo.at[32:40], h_send.at[2], h_recv.at[2], (down, right)
    )
    corner_copy.start()

    own_z.wait()
    for copy in z_copies:
        copy.wait_recv()
    o, c = iota((96, 128), 0), iota((96, 128), 1)
    pack = onehot((o == 6 * (c >> 3) + (c & 7)) & ((c & 7) < 6)).astype(BF16)
    rings[y_at] = dot(pack, wz[...].reshape(128, PAIR)).astype(BF16)

    def y_copy(i, start, size, behind, step):
        piece = rings.at[lax.rem(y_at - behind + NY, NY), start : start + size]
        return remote(piece, piece, y_send.at[i], y_recv.at[i], along_y(step))

    y_near = [y_copy(i, 0, 96, 0, step) for i, step in enumerate((2, -2, 1, -1))]
    for copy in y_near:
        copy.start()

    to_right.wait_recv()
    on_right = cw_copy(2, left, 0, 144, (row, right))
    on_right.start()
    sib_left = cw_copy(4, left, 0, 288, sibling)
    sib_left.start()
    to_left.wait_recv()
    on_left = cw_copy(3, right, 144, 144, (row, left))
    on_left.start()
    sib_right = cw_copy(5, right, 0, 288, sibling)
    sib_right.start()

    lane, sub = iota((8, 256), 1), iota((8, 256), 0)
    for h in range(2):
        blocks = []
        for p in range(4):
            for i in range(8):
                target = i * 32 + ((p - phase[8 * h + i, 0]) & 3) * 8
                blocks.append(onehot(lane == sub + target))
        order = jnp.concatenate(blocks, axis=0).astype(BF16)
        orders[h] = order
        j, c = iota((32, 256), 0), iota((32, 256), 1)
        pick = onehot(j == 4 * (c & 7) + ((c >> 3) & 3)).astype(BF16)
        live = dot(tissue[8 * h : 8 * h + 8, :].astype(F32).astype(BF16), pick)
        live = jnp.where(sub == (lane >> 5), live, 0.0).astype(BF16)
        live = dot(jnp.ones((8, 8), BF16), live).astype(BF16)
        flags[0, 0, :, 256 * h : 256 * h + 256] = dot_nt(live, order).astype(BF16)
    g_copies = []
    for dz in range(4):
        for dc in range(2):
            if dz or dc:
                n = 2 * dz + dc
                peer = row + 2 * (lax.rem(place + dz, 4) - place) + dc * (1 - 2 * core)
                copy = remote(
                    flags.at[0, 0], flags.at[(4 - dz) % 4, dc], g_send.at[n], g_recv.at[n], (peer, col)
                )
                copy.start()
                g_copies.append(copy)

    p32 = proj[...].astype(F32)
    mean_col = jnp.mean(p32, axis=1, keepdims=True)
    mean_row = dot_nt(jnp.ones((8, 768), BF16), proj[...])[0:1] * (1.0 / 768.0)
    gram[...] = (dot_nt(proj[...], proj[...]) * (1.0 / 768.0) - mean_col * mean_row).astype(BF16)

    top_copy.wait_recv()
    left_copy.wait_recv()
    corner_copy.wait_recv()
    inside = row > 0
    inner = col > 0
    o, c = iota((64, 64), 0), iota((64, 64), 1)
    split_row = onehot(c == 8 * (o & 7) + 2 * ((o >> 3) & 3) + (o >> 5)).astype(BF16)
    yt = jnp.where(inside, dot(split_row, top[...]), 0.0).reshape(2, 4, 8, 256)
    grid_in[1, 0, 0, 0:4] = yt[0]
    grid_in[1, 0, 1, 1:5] = yt[1]
    o, c = iota((264, 40), 0), iota((264, 40), 1)
    source = o >> 3
    source = jnp.where(source < 16, source, jnp.where(source == 16, 39, source - 1))
    spread = onehot((c == source) & ((o & 7) == 0)).astype(BF16)
    edge = jnp.where(inner, dot(spread, halo[...]), 0.0).reshape(33, 8, 256)
    first = iota((1, 8, 256), 1) == 0
    moved = pltpu.roll(grid_in[0, 0:16, 1, 4], 1, 1)
    grid_in[0, 0:16, 1, 0] = jnp.where(first, edge[0:16], moved)
    moved = pltpu.roll(grid_in[1, 0:17, 1, 4], 1, 1)
    keep = edge[16:33]
    keep = jnp.where((iota((17, 8, 256), 0) == 0) & jnp.logical_not(inside), 0.0, keep)
    grid_in[1, 0:17, 1, 0] = jnp.where(first, keep, moved)

    on_right.wait_recv()
    sib_on = cw_copy(6, across, 0, 144, sibling)
    sib_on.start()
    on_left.wait_recv()
    sib_off = cw_copy(7, across, 144, 144, sibling)
    sib_off.start()
    own_cw.wait()
    for copy in (sib_left, sib_right, sib_on, sib_off):
        copy.wait_recv()

    y_near[0].wait_recv()
    y_far = [y_copy(4, 0, 96, 2, 1), y_copy(6, 0, 48, 2, 2)]
    for copy in y_far:
        copy.start()
    y_near[1].wait_recv()
    y_back = [y_copy(5, 0, 96, -2, -1), y_copy(7, 48, 48, -2, -2)]
    for copy in y_back:
        copy.start()
    y_far = y_far + y_back

    weights = cwg[...].reshape(2304, 256)
    for h in range(2):
        pieces = []
        for a in range(3):
            for b in range(3):
                rp, i0 = (0, 0) if a == 1 else (1, a // 2)
                sp, m0 = (0, 0) if b == 1 else (1, b // 2)
                window = grid_in[rp, i0 + 8 * h : i0 + 8 * h + 8, sp, m0 : m0 + 4]
                pieces.append(window.reshape(256, 256).astype(BF16))
        pre = dot(jnp.concatenate(pieces, axis=1), weights) + bias[...]
        features = jax.nn.gelu(pre).astype(BF16)
        f32 = features.astype(F32)
        spread_rows = jnp.sum(dot(features, gram[...]) * f32, axis=1, keepdims=True)
        f32 = f32 * lax.rsqrt(jnp.maximum(spread_rows, 0.0) + 1e-05)
        placed = dot(orders[h], f32.astype(BF16)).astype(BF16).reshape(4, 64, 256)
        slots[0, 0, :, 64 * h : 64 * h + 64, :] = placed

    def f_right(p):
        return remote(
            slots.at[0, 0, p], slots.at[3, 0, p], f_send.at[0, p], f_recv.at[3, p],
            (lax.rem(row + 2, ROWS), col),
        )

    def f_left(p):
        return remote(
            slots.at[0, 0, p], slots.at[1, 0, p], f_send.at[1, p], f_recv.at[1, p],
            (lax.rem(row + ROWS - 2, ROWS), col),
        )

    def f_two(p):
        return remote(
            slots.at[0, 0, p], slots.at[2, 0, p], f_send.at[2, p], f_recv.at[2, p],
            (row + 4 * jnp.where(place < 2, 1, -1), col),
        )

    def f_far(p):
        to = jnp.where(place == 2, 1, 3)
        return remote(
            slots.at[2, 0, p], slots.at[to, 0, p], f_send.at[3, p], f_recv.at[to, p],
            (row + 2 * jnp.where(place == 2, 1, -1), col),
        )

    def f_sib(slot, p):
        piece = slots.at[slot, 0, p]
        return remote(piece, slots.at[slot, 1, p], s_send.at[slot, p], s_recv.at[slot, p], sibling)

    def arrived(slot, p):
        piece = slots.at[slot, 0, p]
        return remote(piece, piece, f_send.at[0, p], f_recv.at[slot, p], sibling)

    for p in range(4):

        @pl.when(place < 3)
        def _():
            f_right(p).start()

        @pl.when(place > 0)
        def _():
            f_left(p).start()

        f_two(p).start()
        f_sib(0, p).start()

    def serve(p):
        arrived(2, p).wait_recv()

        @pl.when((place == 1) | (place == 2))
        def _():
            f_far(p).start()

        f_sib(2, p).start()
        for slot in (1, 3):
            arrived(slot, p).wait_recv()
            f_sib(slot, p).start()

    for copy in y_near[2:] + y_far:
        copy.wait_recv()
    w = rings[...].reshape(768, PAIR)
    folded = dot(proj[...], w) - mean_col * dot(jnp.ones((8, 768), BF16), w)[0:1]
    scale = jnp.where(iota((1, PAIR), 1) < 128, 0.125 * 1.4426950408889634, 1.0)
    fold[group] = (folded * scale).astype(BF16)

    x_copies = [
        (a, remote(fold.at[a % 3], fold.at[a % 3], x_send.at[b], x_recv.at[a % 3], (row, b)))
        for a, b in ((0, 1), (1, 0), (1, 2), (1, 3), (2, 1), (2, 3), (2, 0), (3, 2))
    ]
    for a, copy in x_copies:
        pl.when(col == a)(copy.start)
    for copy in g_copies:
        copy.wait_recv()
    lane128 = iota((512, 128), 1)
    first_row = onehot((iota((8, 128), 0) == 0) & (iota((8, 128), 1) == 0)).astype(BF16)
    for q in range(4):
        for c in range(2):
            live = dot_tn(flags[q, c], first_row)
            gone = jnp.where((lane128 == 0) , (live - 1.0) * 1e30, 0.0).astype(BF16)
            gone = gone.reshape(2, 4, 64, 128)
            for h in range(2):
                dead[:, q, c, 64 * h : 64 * h + 64, :] = gone[h]

    serve(0)
    lane = iota((256, 128), 1)
    unit = onehot(iota((512, 128), 1) == 0).astype(BF16)
    ones = jnp.ones((16, 1024), BF16)

    def give(p):
        return remote(mixed.at[p, :, 128:256], theirs.at[p], m_send.at[p], m_recv.at[p], sibling)

    def item(p, n):
        x = slots[:, :, p].reshape(1024, 256)
        mask = dead[p].reshape(1024, 128)
        kv = dot(x, fold[n, :, 128:384])
        keys = jnp.concatenate([kv[:, 0:128].astype(BF16), mask], axis=1)
        values = jnp.concatenate([kv[:, 128:256].T.astype(BF16), ones], axis=0)
        q_pair = dot(x[0:256], fold[n, :, 0:128])
        heads = jnp.concatenate(
            [jnp.where(lane < 64, q_pair, 0.0), jnp.where(lane < 64, 0.0, q_pair)], axis=0
        ).astype(BF16)
        scores = dot_nt(keys, jnp.concatenate([heads, unit], axis=1))
        highest = jnp.max(scores, axis=0, keepdims=True)
        weights = jnp.exp2(scores - highest).astype(BF16)
        result = dot(values, weights)
        result = result[0:128] / result[128:129]
        upper = iota((128, 256), 0) < 64
        mixed[p, n] = jnp.where(upper, result[:, 0:256], result[:, 256:512]).T.astype(BF16)

    def first(p):
        for slot in range(4):
            f_sib(slot, p).wait_recv()
        item(p, group)

    def early(p, carry):
        first(p)

        @pl.when(p == 0)
        def _():
            serve(1)

        return carry

    lax.fori_loop(0, 2, early, 0)

    for g in range(3):
        pl.when(group != g)(remote(
            fold.at[g], fold.at[g], x_send.at[0], x_recv.at[g], sibling
        ).wait_recv)

    def late(p, carry):
        serve(p + 2)
        for k in (1, 2):
            item(p, lax.rem(group + k, 3))
        give(p).start()
        return carry

    lax.fori_loop(0, 2, late, 0)

    def last(p, carry):
        for slot in range(4):
            f_sib(slot, p).wait_recv()
        for k in range(3):
            item(p, lax.rem(group + k, 3))
        give(p).start()
        return carry

    lax.fori_loop(2, 4, last, 0)

    back = []
    j, lane = iota((32, 256), 0), iota((32, 256), 1)
    for h in range(2):
        blocks = []
        for i in range(8):
            p = ((j & 3) + phase[8 * h + i, 0]) & 3
            blocks.append(onehot(lane == p * 64 + i * 8 + (j >> 2)))
        live = flags[0, 0, 0:1, 256 * h : 256 * h + 256].astype(F32)
        back.append((jnp.concatenate(blocks, axis=0) * live).astype(BF16))
    for p in range(4):
        give(p).wait_recv()
    for h in range(2):
        a, b = (
            jnp.concatenate(
                [dot(back[h], m[:, n, 64 * h : 64 * h + 64].reshape(256, 128)) for n in range(3)],
                axis=1,
            )
            for m in (mixed, theirs)
        )
        lower = jnp.where(core == 0, a, b).astype(BF16).reshape(8, 32, 384)
        upper = jnp.where(core == 0, b, a).astype(BF16).reshape(8, 32, 384)
        out[8 * h : 8 * h + 8, :, 0:384] = lower
        out[8 * h : 8 * h + 8, :, 384:768] = upper

    for copy in z_copies + g_copies + [
        to_right, to_left, on_right, on_left, sib_left, sib_right, sib_on, sib_off,
        top_copy, left_copy, corner_copy,
    ]:
        copy.wait_send()
    for copy in y_near + y_far:
        copy.wait_send()
    for a, copy in x_copies:
        pl.when(col == a)(copy.wait_send)
    for p in range(4):
        give(p).wait_send()
        f_two(p).wait_send()
        for slot in range(4):
            f_sib(slot, p).wait_send()

        @pl.when(place < 3)
        def _():
            f_right(p).wait_send()

        @pl.when(place > 0)
        def _():
            f_left(p).wait_send()

        @pl.when((place == 1) | (place == 2))
        def _():
            f_far(p).wait_send()


def local(feat_in, conv_weight, conv_bias, proj_weight, qkv_weight, tissue, phase):
    vmem = pl.BlockSpec(memory_space=pltpu.VMEM)
    dma = pltpu.SemaphoreType.DMA
    return pl.pallas_call(
        whole_kernel,
        out_shape=jax.ShapeDtypeStruct((16, 32, 768), BF16),
        in_specs=[vmem] * 5 + [pl.BlockSpec(memory_space=pltpu.SMEM), vmem],
        out_specs=vmem,
        scratch_shapes=[
            pltpu.VMEM((2, 17, 2, 5, 8, 256), F32),
            pltpu.VMEM((32, 256), BF16),
            pltpu.VMEM((40, 256), BF16),
            pltpu.VMEM((64, 256), BF16),
            pltpu.VMEM((4, 576, 256), BF16),
            pltpu.VMEM((2, 8, PAIR), BF16),
            pltpu.VMEM((16, 8, PAIR), BF16),
            pltpu.VMEM((NY, 96, PAIR), BF16),
            pltpu.VMEM((4, 2, 4, 128, 256), BF16),
            pltpu.VMEM((4, 2, 8, 512), BF16),
            pltpu.VMEM((2, 256, 256), BF16),
            pltpu.VMEM((3, 256, PAIR), BF16),
            pltpu.VMEM((256, 256), BF16),
            pltpu.VMEM((4, 4, 2, 128, 128), BF16),
            pltpu.VMEM((4, 3, 256, 128), BF16),
            pltpu.VMEM((4, 3, 128, 128), BF16),
            dma((8,)), dma((8,)),
            dma((3,)), dma((3,)),
            dma((16,)), dma((16,)),
            dma((8,)), dma((8,)),
            dma((4, 4)), dma((4, 4)),
            dma((4, 4)), dma((4, 4)),
            dma((8,)), dma((8,)),
            dma((4,)), dma((3,)),
            dma((4,)), dma((4,)),
            dma((2,)),
        ],
        compiler_params=pltpu.CompilerParams(
            collective_id=0, has_side_effects=True, vmem_limit_bytes=VMEM_LIMIT
        ),
        name="whole",
    )(
        feat_in, conv_weight, conv_bias.reshape(1, 256), qkv_weight, proj_weight, phase, tissue
    )


def solution(mesh):
    in_specs = (
        P("row", "col", None),
        P("col", None),
        P(),
        P(),
        P("row", None),
        P("row", "col"),
        P("row", "col"),
    )
    out_specs = P("row", "col", None)
    return jax.shard_map(local, mesh=mesh, in_specs=in_specs, out_specs=out_specs, check_vma=False)
```

```python
import jax
import jax.numpy as jnp
from jax import lax
from jax.experimental import pallas as pl
from jax.experimental.pallas import tpu as pltpu
from jax.sharding import PartitionSpec as P

MESH = pl.DeviceIdType.MESH
F32 = jnp.float32
BF16 = jnp.bfloat16
ROWS = 128
COLS = 4
PLANE = 16
NY = 8
PAIR = 384
VMEM_LIMIT = 56 * 1024 * 1024


def iota(shape, dim):
    return lax.broadcasted_iota(jnp.int32, shape, dim)


def onehot(cond):
    return jnp.where(cond, 1.0, 0.0)


def dot(a, b):
    return jnp.dot(a, b, preferred_element_type=F32)


def dot_nt(a, b):
    return lax.dot_general(a, b, (((1,), (1,)), ((), ())), preferred_element_type=F32)


def dot_tn(a, b):
    return lax.dot_general(a, b, (((0,), (0,)), ((), ())), preferred_element_type=F32)


def remote(src, dst, send_sem, recv_sem, device):
    return pltpu.make_async_remote_copy(
        src_ref=src,
        dst_ref=dst,
        send_sem=send_sem,
        recv_sem=recv_sem,
        device_id=device,
        device_id_type=MESH,
    )


def greet(devices):
    barrier = pltpu.get_barrier_semaphore()
    for device in devices:
        pl.semaphore_signal(barrier, inc=1, device_id=device, device_id_type=MESH)
    pl.semaphore_wait(barrier, len(devices))


def whole_kernel(
    feat, cw, bias, w6, proj, phase, tissue, out,
    grid_in, ext, halo, top, cwg, wsend, wz, rings, slots, flags, orders,
    fold, gram, dead, mixed, theirs,
    cw_send, cw_recv, h_send, h_recv, z_send, z_recv, g_send, g_recv,
    f_send, f_recv, s_send, s_recv, y_send, y_recv, x_send, x_recv, m_send, m_recv, own_sem,
):
    row, col = lax.axis_index("row"), lax.axis_index("col")
    core = lax.rem(row, 2)
    base = row - lax.rem(row, PLANE)
    mine = row - base
    y_at = row // PLANE
    place = lax.rem(row // 2, 4)
    sibling = (row + 1 - 2 * core, col)
    right, left = lax.rem(col + 1, COLS), lax.rem(col + COLS - 1, COLS)
    across = lax.rem(col + 2, COLS)
    down, up = lax.rem(row + 1, ROWS), lax.rem(row + ROWS - 1, ROWS)

    def along_y(step):
        return (lax.rem(row + PLANE * step + ROWS, ROWS), col)

    plane = [(base + lax.rem(mine + k, PLANE), col) for k in range(1, PLANE)]
    greet(
        [(row, right), (row, left), (down, col), (up, col), (down, right), (up, left)]
        + [(row, across)]
        + [along_y(step) for step in (1, -1, 2, -2)]
        + plane
    )

    part = pl.multiple_of(core * 288, 32)

    def cw_piece(slot, start, size):
        return cwg.at[slot, pl.ds(pl.multiple_of(part + start, 16), size), :]

    def cw_copy(i, slot, start, size, device):
        piece = cw_piece(slot, start, size)
        return remote(piece, piece, cw_send.at[i], cw_recv.at[i], device)

    own_cw = pltpu.make_async_copy(cw, cwg.at[col], own_sem.at[0])
    own_cw.start()
    half = cw.at[pl.ds(part, 288), :]
    to_right = remote(half, cw_piece(col, 0, 288), cw_send.at[0], cw_recv.at[0], (row, right))
    to_left = remote(half, cw_piece(col, 0, 288), cw_send.at[1], cw_recv.at[1], (row, left))
    to_right.start()
    to_left.start()
    top_copy = remote(feat.at[31], top, h_send.at[0], h_recv.at[0], (down, col))
    top_copy.start()

    group = lax.rem(col, 3)
    for c in range(2):
        wsend[c] = jnp.zeros((8, PAIR), BF16)
        for j in range(3):
            at = pl.multiple_of(768 * j + 384 * c + 128 * group, 128)
            wsend[c, 0:6, 128 * j : 128 * j + 128] = w6[:, pl.ds(at, 128)]
    z_copies = []
    for k in range(1, PLANE):
        to_core = lax.rem(core + k, 2)
        copy = remote(
            wsend.at[to_core], wz.at[mine], z_send.at[k], z_recv.at[k], plane[k - 1]
        )
        copy.start()
        z_copies.append(copy)
    own_z = pltpu.make_async_copy(wsend.at[core], wz.at[mine], own_sem.at[1])
    own_z.start()

    o, c = iota((256, 256), 0), iota((256, 256), 1)
    k, si, sp = o & 7, (o >> 3) & 3, (o >> 5) & 1
    r = 2 * ((o >> 6) & 1) + (o >> 7)
    split = onehot(c == r * 64 + 8 * k + 2 * si + sp).astype(BF16)
    for g in range(8):
        x = feat[4 * g : 4 * g + 4].reshape(256, 256)
        y = dot(split, x).reshape(2, 2, 2, 4, 8, 256)
        grid_in[0, 2 * g : 2 * g + 2, 0, 0:4] = y[0, :, 0]
        grid_in[0, 2 * g : 2 * g + 2, 1, 1:5] = y[0, :, 1]
        grid_in[1, 2 * g + 1 : 2 * g + 3, 0, 0:4] = y[1, :, 0]
        grid_in[1, 2 * g + 1 : 2 * g + 3, 1, 1:5] = y[1, :, 1]

    for rp in range(2):
        for i in range(0, 16, 8):
            rows8 = [grid_in[rp, rp + i + e, 1, 4, 7:8, :] for e in range(8)]
            ext[16 * rp + i : 16 * rp + i + 8, :] = jnp.concatenate(rows8, axis=0).astype(BF16)
    left_copy = remote(ext, halo.at[0:32], h_send.at[1], h_recv.at[1], (row, right))
    left_copy.start()
    corner_copy = remote(
        ext.at[24:32], halo.at[32:40], h_send.at[2], h_recv.at[2], (down, right)
    )
    corner_copy.start()

    own_z.wait()
    for copy in z_copies:
        copy.wait_recv()
    o, c = iota((96, 128), 0), iota((96, 128), 1)
    pack = onehot((o == 6 * (c >> 3) + (c & 7)) & ((c & 7) < 6)).astype(BF16)
    rings[y_at] = dot(pack, wz[...].reshape(128, PAIR)).astype(BF16)

    def y_copy(i, start, size, behind, step):
        piece = rings.at[lax.rem(y_at - behind + NY, NY), start : start + size]
        return remote(piece, piece, y_send.at[i], y_recv.at[i], along_y(step))

    y_near = [y_copy(i, 0, 96, 0, step) for i, step in enumerate((2, -2, 1, -1))]
    for copy in y_near:
        copy.start()

    to_right.wait_recv()
    on_right = cw_copy(2, left, 0, 144, (row, right))
    on_right.start()
    sib_left = cw_copy(4, left, 0, 288, sibling)
    sib_left.start()
    to_left.wait_recv()
    on_left = cw_copy(3, right, 144, 144, (row, left))
    on_left.start()
    sib_right = cw_copy(5, right, 0, 288, sibling)
    sib_right.start()

    lane, sub = iota((8, 256), 1), iota((8, 256), 0)
    for h in range(2):
        blocks = []
        for p in range(4):
            for i in range(8):
                target = i * 32 + ((p - phase[8 * h + i, 0]) & 3) * 8
                blocks.append(onehot(lane == sub + target))
        order = jnp.concatenate(blocks, axis=0).astype(BF16)
        orders[h] = order
        j, c = iota((32, 256), 0), iota((32, 256), 1)
        pick = onehot(j == 4 * (c & 7) + ((c >> 3) & 3)).astype(BF16)
        live = dot(tissue[8 * h : 8 * h + 8, :].astype(F32).astype(BF16), pick)
        live = jnp.where(sub == (lane >> 5), live, 0.0).astype(BF16)
        live = dot(jnp.ones((8, 8), BF16), live).astype(BF16)
        flags[0, 0, :, 256 * h : 256 * h + 256] = dot_nt(live, order).astype(BF16)
    g_copies = []
    for dz in range(4):
        for dc in range(2):
            if dz or dc:
                n = 2 * dz + dc
                peer = row + 2 * (lax.rem(place + dz, 4) - place) + dc * (1 - 2 * core)
                copy = remote(
                    flags.at[0, 0], flags.at[(4 - dz) % 4, dc], g_send.at[n], g_recv.at[n], (peer, col)
                )
                copy.start()
                g_copies.append(copy)

    p32 = proj[...].astype(F32)
    mean_col = jnp.mean(p32, axis=1, keepdims=True)
    mean_row = dot_nt(jnp.ones((8, 768), BF16), proj[...])[0:1] * (1.0 / 768.0)
    gram[...] = (dot_nt(proj[...], proj[...]) * (1.0 / 768.0) - mean_col * mean_row).astype(BF16)

    top_copy.wait_recv()
    left_copy.wait_recv()
    corner_copy.wait_recv()
    inside = row > 0
    inner = col > 0
    o, c = iota((64, 64), 0), iota((64, 64), 1)
    split_row = onehot(c == 8 * (o & 7) + 2 * ((o >> 3) & 3) + (o >> 5)).astype(BF16)
    yt = jnp.where(inside, dot(split_row, top[...]), 0.0).reshape(2, 4, 8, 256)
    grid_in[1, 0, 0, 0:4] = yt[0]
    grid_in[1, 0, 1, 1:5] = yt[1]
    o, c = iota((264, 40), 0), iota((264, 40), 1)
    source = o >> 3
    source = jnp.where(source < 16, source, jnp.where(source == 16, 39, source - 1))
    spread = onehot((c == source) & ((o & 7) == 0)).astype(BF16)
    edge = jnp.where(inner, dot(spread, halo[...]), 0.0).reshape(33, 8, 256)
    first = iota((1, 8, 256), 1) == 0
    moved = pltpu.roll(grid_in[0, 0:16, 1, 4], 1, 1)
    grid_in[0, 0:16, 1, 0] = jnp.where(first, edge[0:16], moved)
    moved = pltpu.roll(grid_in[1, 0:17, 1, 4], 1, 1)
    keep = edge[16:33]
    keep = jnp.where((iota((17, 8, 256), 0) == 0) & jnp.logical_not(inside), 0.0, keep)
    grid_in[1, 0:17, 1, 0] = jnp.where(first, keep, moved)

    on_right.wait_recv()
    sib_on = cw_copy(6, across, 0, 144, sibling)
    sib_on.start()
    on_left.wait_recv()
    sib_off = cw_copy(7, across, 144, 144, sibling)
    sib_off.start()
    own_cw.wait()
    for copy in (sib_left, sib_right, sib_on, sib_off):
        copy.wait_recv()

    y_near[0].wait_recv()
    y_far = [y_copy(4, 0, 96, 2, 1), y_copy(6, 0, 48, 2, 2)]
    for copy in y_far:
        copy.start()
    y_near[1].wait_recv()
    y_back = [y_copy(5, 0, 96, -2, -1), y_copy(7, 48, 48, -2, -2)]
    for copy in y_back:
        copy.start()
    y_far = y_far + y_back

    weights = cwg[...].reshape(2304, 256)
    for h in range(2):
        pieces = []
        for a in range(3):
            for b in range(3):
                rp, i0 = (0, 0) if a == 1 else (1, a // 2)
                sp, m0 = (0, 0) if b == 1 else (1, b // 2)
                window = grid_in[rp, i0 + 8 * h : i0 + 8 * h + 8, sp, m0 : m0 + 4]
                pieces.append(window.reshape(256, 256).astype(BF16))
        pre = dot(jnp.concatenate(pieces, axis=1), weights) + bias[...]
        features = jax.nn.gelu(pre).astype(BF16)
        f32 = features.astype(F32)
        spread_rows = jnp.sum(dot(features, gram[...]) * f32, axis=1, keepdims=True)
        f32 = f32 * lax.rsqrt(jnp.maximum(spread_rows, 0.0) + 1e-05)
        placed = dot(orders[h], f32.astype(BF16)).astype(BF16).reshape(4, 64, 256)
        slots[0, 0, :, 64 * h : 64 * h + 64, :] = placed

    def f_right(p):
        return remote(
            slots.at[0, 0, p], slots.at[3, 0, p], f_send.at[0, p], f_recv.at[3, p],
            (lax.rem(row + 2, ROWS), col),
        )

    def f_left(p):
        return remote(
            slots.at[0, 0, p], slots.at[1, 0, p], f_send.at[1, p], f_recv.at[1, p],
            (lax.rem(row + ROWS - 2, ROWS), col),
        )

    def f_two(p):
        return remote(
            slots.at[0, 0, p], slots.at[2, 0, p], f_send.at[2, p], f_recv.at[2, p],
            (row + 4 * jnp.where(place < 2, 1, -1), col),
        )

    def f_far(p):
        to = jnp.where(place == 2, 1, 3)
        return remote(
            slots.at[2, 0, p], slots.at[to, 0, p], f_send.at[3, p], f_recv.at[to, p],
            (row + 2 * jnp.where(place == 2, 1, -1), col),
        )

    def f_sib(slot, p):
        piece = slots.at[slot, 0, p]
        return remote(piece, slots.at[slot, 1, p], s_send.at[slot, p], s_recv.at[slot, p], sibling)

    def arrived(slot, p):
        piece = slots.at[slot, 0, p]
        return remote(piece, piece, f_send.at[0, p], f_recv.at[slot, p], sibling)

    for p in range(4):
        f_two(p).start()

        @pl.when(place < 3)
        def _():
            f_right(p).start()

        @pl.when(place > 0)
        def _():
            f_left(p).start()

        f_sib(0, p).start()

    def serve(p):
        arrived(2, p).wait_recv()

        @pl.when((place == 1) | (place == 2))
        def _():
            f_far(p).start()

        f_sib(2, p).start()
        for slot in (1, 3):
            arrived(slot, p).wait_recv()
            f_sib(slot, p).start()

    for copy in y_near[2:] + y_far:
        copy.wait_recv()
    w = rings[...].reshape(768, PAIR)
    folded = dot(proj[...], w) - mean_col * dot(jnp.ones((8, 768), BF16), w)[0:1]
    scale = jnp.where(iota((1, PAIR), 1) < 128, 0.125 * 1.4426950408889634, 1.0)
    fold[group] = (folded * scale).astype(BF16)

    x_copies = [
        (a, remote(fold.at[a % 3], fold.at[a % 3], x_send.at[b], x_recv.at[a % 3], (row, b)))
        for a, b in ((0, 1), (1, 0), (1, 2), (1, 3), (2, 1), (2, 3), (2, 0), (3, 2))
    ]
    for a, copy in x_copies:
        pl.when(col == a)(copy.start)
    for copy in g_copies:
        copy.wait_recv()
    lane128 = iota((512, 128), 1)
    first_row = onehot((iota((8, 128), 0) == 0) & (iota((8, 128), 1) == 0)).astype(BF16)
    for q in range(4):
        for c in range(2):
            live = dot_tn(flags[q, c], first_row)
            gone = jnp.where((lane128 == 0) , (live - 1.0) * 1e30, 0.0).astype(BF16)
            gone = gone.reshape(2, 4, 64, 128)
            for h in range(2):
                dead[:, q, c, 64 * h : 64 * h + 64, :] = gone[h]

    serve(0)
    lane = iota((256, 128), 1)
    unit = onehot(iota((512, 128), 1) == 0).astype(BF16)
    ones = jnp.ones((16, 1024), BF16)

    def give(p):
        return remote(mixed.at[p, :, 128:256], theirs.at[p], m_send.at[p], m_recv.at[p], sibling)

    def item(p, n):
        x = slots[:, :, p].reshape(1024, 256)
        mask = dead[p].reshape(1024, 128)
        kv = dot(x, fold[n, :, 128:384])
        keys = jnp.concatenate([kv[:, 0:128].astype(BF16), mask], axis=1)
        values = jnp.concatenate([kv[:, 128:256].T.astype(BF16), ones], axis=0)
        q_pair = dot(x[0:256], fold[n, :, 0:128])
        heads = jnp.concatenate(
            [jnp.where(lane < 64, q_pair, 0.0), jnp.where(lane < 64, 0.0, q_pair)], axis=0
        ).astype(BF16)
        scores = dot_nt(keys, jnp.concatenate([heads, unit], axis=1))
        highest = jnp.max(scores, axis=0, keepdims=True)
        weights = jnp.exp2(scores - highest).astype(BF16)
        result = dot(values, weights)
        result = result[0:128] / result[128:129]
        upper = iota((128, 256), 0) < 64
        mixed[p, n] = jnp.where(upper, result[:, 0:256], result[:, 256:512]).T.astype(BF16)

    def first(p):
        for slot in range(4):
            f_sib(slot, p).wait_recv()
        item(p, group)

    def early(p, carry):
        first(p)

        @pl.when(p == 0)
        def _():
            serve(1)

        return carry

    lax.fori_loop(0, 2, early, 0)

    for g in range(3):
        pl.when(group != g)(remote(
            fold.at[g], fold.at[g], x_send.at[0], x_recv.at[g], sibling
        ).wait_recv)

    def late(p, carry):
        serve(p + 2)
        for k in (1, 2):
            item(p, lax.rem(group + k, 3))
        give(p).start()
        return carry

    lax.fori_loop(0, 2, late, 0)

    def last(p, carry):
        for slot in range(4):
            f_sib(slot, p).wait_recv()
        for k in range(3):
            item(p, lax.rem(group + k, 3))
        give(p).start()
        return carry

    lax.fori_loop(2, 4, last, 0)

    back = []
    j, lane = iota((32, 256), 0), iota((32, 256), 1)
    for h in range(2):
        blocks = []
        for i in range(8):
            p = ((j & 3) + phase[8 * h + i, 0]) & 3
            blocks.append(onehot(lane == p * 64 + i * 8 + (j >> 2)))
        live = flags[0, 0, 0:1, 256 * h : 256 * h + 256].astype(F32)
        back.append((jnp.concatenate(blocks, axis=0) * live).astype(BF16))
    for p in range(4):
        give(p).wait_recv()
    for h in range(2):
        a, b = (
            jnp.concatenate(
                [dot(back[h], m[:, n, 64 * h : 64 * h + 64].reshape(256, 128)) for n in range(3)],
                axis=1,
            )
            for m in (mixed, theirs)
        )
        lower = jnp.where(core == 0, a, b).astype(BF16).reshape(8, 32, 384)
        upper = jnp.where(core == 0, b, a).astype(BF16).reshape(8, 32, 384)
        out[8 * h : 8 * h + 8, :, 0:384] = lower
        out[8 * h : 8 * h + 8, :, 384:768] = upper

    for copy in z_copies + g_copies + [
        to_right, to_left, on_right, on_left, sib_left, sib_right, sib_on, sib_off,
        top_copy, left_copy, corner_copy,
    ]:
        copy.wait_send()
    for copy in y_near + y_far:
        copy.wait_send()
    for a, copy in x_copies:
        pl.when(col == a)(copy.wait_send)
    for p in range(4):
        give(p).wait_send()
        f_two(p).wait_send()
        for slot in range(4):
            f_sib(slot, p).wait_send()

        @pl.when(place < 3)
        def _():
            f_right(p).wait_send()

        @pl.when(place > 0)
        def _():
            f_left(p).wait_send()

        @pl.when((place == 1) | (place == 2))
        def _():
            f_far(p).wait_send()


def local(feat_in, conv_weight, conv_bias, proj_weight, qkv_weight, tissue, phase):
    vmem = pl.BlockSpec(memory_space=pltpu.VMEM)
    dma = pltpu.SemaphoreType.DMA
    return pl.pallas_call(
        whole_kernel,
        out_shape=jax.ShapeDtypeStruct((16, 32, 768), BF16),
        in_specs=[vmem] * 5 + [pl.BlockSpec(memory_space=pltpu.SMEM), vmem],
        out_specs=vmem,
        scratch_shapes=[
            pltpu.VMEM((2, 17, 2, 5, 8, 256), F32),
            pltpu.VMEM((32, 256), BF16),
            pltpu.VMEM((40, 256), BF16),
            pltpu.VMEM((64, 256), BF16),
            pltpu.VMEM((4, 576, 256), BF16),
            pltpu.VMEM((2, 8, PAIR), BF16),
            pltpu.VMEM((16, 8, PAIR), BF16),
            pltpu.VMEM((NY, 96, PAIR), BF16),
            pltpu.VMEM((4, 2, 4, 128, 256), BF16),
            pltpu.VMEM((4, 2, 8, 512), BF16),
            pltpu.VMEM((2, 256, 256), BF16),
            pltpu.VMEM((3, 256, PAIR), BF16),
            pltpu.VMEM((256, 256), BF16),
            pltpu.VMEM((4, 4, 2, 128, 128), BF16),
            pltpu.VMEM((4, 3, 256, 128), BF16),
            pltpu.VMEM((4, 3, 128, 128), BF16),
            dma((8,)), dma((8,)),
            dma((3,)), dma((3,)),
            dma((16,)), dma((16,)),
            dma((8,)), dma((8,)),
            dma((4, 4)), dma((4, 4)),
            dma((4, 4)), dma((4, 4)),
            dma((8,)), dma((8,)),
            dma((4,)), dma((3,)),
            dma((4,)), dma((4,)),
            dma((2,)),
        ],
        compiler_params=pltpu.CompilerParams(
            collective_id=0, has_side_effects=True, vmem_limit_bytes=VMEM_LIMIT
        ),
        name="whole",
    )(
        feat_in, conv_weight, conv_bias.reshape(1, 256), qkv_weight, proj_weight, phase, tissue
    )


def solution(mesh):
    in_specs = (
        P("row", "col", None),
        P("col", None),
        P(),
        P(),
        P("row", None),
        P("row", "col"),
        P("row", "col"),
    )
    out_specs = P("row", "col", None)
    return jax.shard_map(local, mesh=mesh, in_specs=in_specs, out_specs=out_specs, check_vma=False)
```
